256 devices in a mesh: shell: 128 (over x, y, z), radial: 2 (over core).
Axes of the slice: x: 4, y: 4, z: 8, core: 2. Of those that a mesh axis runs over, the one named last changes fastest.
Arguments:
- state: float32 [8, 32, 1024, 128], P(None, 'radial', 'shell')
- footpoints: int32 [32, 1024, 128], P('radial', 'shell'), may hold values from 0 to 32767, as said below
- conductance: float32 [4, 128, 256], P(None, 'shell', 'radial'), may hold values from 0.1 to 0.45
- inverse_blocks: float32 [128, 2, 128, 128], P('shell', 'radial')
Outputs:
- state_next: float32 [8, 32, 1024, 128], P(None, 'radial', 'shell')
- potential: float32 [128, 256], P('shell', 'radial')
- footpoint_potential: float32 [32, 1024, 128], P('radial', 'shell')
The draws below stay inside these ranges and needn't reach their ends.
Inputs may be any that keep to these rules, and one draw needn't show every extreme that they name: `footpoints`: A cell whose longitude index lon lies in shell block s = lon // 8 maps to a node whose column (node % 256) lies in s * 2 to (s + 1) * 2 - 1.
All inputs are finite; a program needn't handle non-finite values.
Results may differ from the reference program's by a relative error of at most 0.0003.
Values sent between devices are 32-bit elements; how exact they have to be, the bound alone decides.
A program may use at most 64 MiB of HBM per device.

```python
import math
import jax
import jax.numpy as jnp
from jax import lax

LON_DEV = 8
LAT_G = 128
NLAT_I = 128
NLON_I = 256
ITERS_I = 4
R_G = 32
LON_G = 1024
LON_SECT = 2
HALVES = 2
HALF = 128


GAMMA = 5.0 / 3.0


def draw_state(key, part):
    subkeys = jax.random.split(jax.random.fold_in(key, 11), 4)
    grid_shape = (R_G, LON_G, LAT_G)
    density = jnp.exp(jax.random.uniform(subkeys[0], grid_shape, jnp.float32, 0.0, math.log(2.0)))
    velocity = jnp.clip(0.3 * jax.random.normal(subkeys[1], (3,) + grid_shape, jnp.float32), -1.0, 1.0)
    magnetic = jnp.clip(0.5 * jax.random.normal(subkeys[2], (3,) + grid_shape, jnp.float32), -2.0, 2.0)
    pressure = jnp.exp(jax.random.uniform(subkeys[3], grid_shape, jnp.float32, math.log(0.5), math.log(2.0)))
    kinetic = jnp.sum(velocity * velocity, axis=0)
    field_sq = jnp.sum(magnetic * magnetic, axis=0)
    energy = pressure / (GAMMA - 1.0) + 0.5 * density * kinetic + 0.5 * field_sq
    return jnp.concatenate([density[None], density[None] * velocity, magnetic, energy[None]], axis=0)


def draw_footpoints(key, part):
    key_lat = jax.random.fold_in(key, 21)
    key_lon = jax.random.fold_in(key, 22)
    grid_shape = (R_G, LON_G, LAT_G)
    radial_cells = lax.broadcasted_iota(jnp.int32, grid_shape, 0)
    lon_cells = lax.broadcasted_iota(jnp.int32, grid_shape, 1)
    lat_cells = lax.broadcasted_iota(jnp.int32, grid_shape, 2)
    column = lon_cells // LON_DEV * LON_SECT + jax.random.randint(key_lon, grid_shape, 0, LON_SECT)
    latitude = lat_cells * NLAT_I // LAT_G + radial_cells * 3 // R_G + jax.random.randint(key_lat, grid_shape, -4, 5)
    latitude = jnp.clip(latitude, 0, NLAT_I - 1)
    node_index = latitude * NLON_I + column
    node_index = node_index.at[0, 0, 0].set(0)
    node_index = node_index.at[R_G - 1, LON_G - 1, LAT_G - 1].set(NLAT_I * NLON_I - 1)
    return node_index.astype(jnp.int32)


def draw_inverse_blocks(key, part):
    key_diag = jax.random.fold_in(key, 31)
    key_off = jax.random.fold_in(key, 32)
    block_shape = (NLAT_I, HALVES, HALF, HALF)
    diagonal = jax.random.uniform(key_diag, (NLAT_I, HALVES, HALF), jnp.float32, 0.5, 1.0)
    spread = jax.random.normal(key_off, block_shape, jnp.float32) * (0.5 / math.sqrt(HALF))
    identity = (lax.broadcasted_iota(jnp.int32, block_shape, 2) == lax.broadcasted_iota(jnp.int32, block_shape, 3)).astype(jnp.float32)
    return spread + identity * diagonal[..., None]


def block_levels(key, shape, cuts, smallest, high):
    level, own = 1.0, jax.random.fold_in(key, 6)
    for dim, parts in cuts:
        heights = jnp.exp(jax.random.uniform(jax.random.fold_in(own, dim), (parts,), jnp.float32, smallest / len(cuts), high / len(cuts)))
        level = level * jnp.repeat(heights, shape[dim] // parts).reshape([-1 if axis == dim else 1 for axis in range(len(shape))])
    return level


def setup_inputs(seed: int = 0) -> dict:
    arg_keys = jax.random.split(jax.random.key(seed), 5)
    return {
        "state": draw_state(jax.random.fold_in(arg_keys[4], 71), 0),
        "footpoints": draw_footpoints(jax.random.fold_in(arg_keys[4], 71), 0),
        "conductance": jnp.clip(jnp.exp(math.log(0.45) - 1.50407736 * jax.random.uniform(arg_keys[2], (4, NLAT_I, NLON_I), jnp.float32) ** block_levels(arg_keys[2], (4, NLAT_I, NLON_I), ((1, 128), (2, 2)), -0.2, 0.2)), 0.1, 0.45),
        "inverse_blocks": draw_inverse_blocks(jax.random.fold_in(arg_keys[4], 71), 0),
    }


GAMMA = 5.0 / 3.0
TIME_STEP = 0.02
CELL_AREA = 0.125

def minmod(first_jump, second_jump):
    return 0.5 * (jnp.sign(first_jump) + jnp.sign(second_jump)) * jnp.minimum(jnp.abs(first_jump), jnp.abs(second_jump))

def physical_flux(conserved, direction):
    density = conserved[0]
    velocity = conserved[1:4] / density
    magnetic = conserved[4:7]
    energy = conserved[7]
    field_sq = lax.optimization_barrier(jnp.sum(magnetic * magnetic, axis=0))
    kinetic = lax.optimization_barrier(jnp.sum(velocity * velocity, axis=0))
    pressure = (GAMMA - 1.0) * (energy - 0.5 * density * kinetic - 0.5 * field_sq)
    total_pressure = pressure + 0.5 * field_sq
    normal_speed = velocity[direction]
    normal_field = magnetic[direction]
    selector = (jnp.arange(3) == direction).astype(jnp.float32).reshape((3,) + (1,) * density.ndim)
    momentum_flux = density * velocity * normal_speed - magnetic * normal_field + total_pressure * selector
    induction = normal_speed * magnetic - normal_field * velocity
    alignment = lax.optimization_barrier(jnp.sum(velocity * magnetic, axis=0))
    energy_flux = (energy + total_pressure) * normal_speed - normal_field * alignment
    fluxes = jnp.concatenate([(density * normal_speed)[None], momentum_flux, induction, energy_flux[None]], axis=0)
    signal = jnp.abs(normal_speed) + jnp.sqrt((GAMMA * jnp.abs(pressure) + field_sq) / density)
    return (fluxes, signal)

def face_divergence(padded, direction):
    dimension = direction + 1
    cell_count = padded.shape[dimension] - 4

    def window_slice(array, first_index, length):
        return lax.slice_in_dim(array, first_index, first_index + length, axis=dimension)
    jumps = window_slice(padded, 1, cell_count + 3) - window_slice(padded, 0, cell_count + 3)
    slopes = minmod(window_slice(jumps, 1, cell_count + 2), window_slice(jumps, 0, cell_count + 2))
    left_state = window_slice(padded, 1, cell_count + 1) + 0.5 * window_slice(slopes, 0, cell_count + 1)
    right_state = window_slice(padded, 2, cell_count + 1) - 0.5 * window_slice(slopes, 1, cell_count + 1)
    left_flux, left_signal = physical_flux(left_state, direction)
    right_flux, right_signal = physical_flux(right_state, direction)
    signal_max = jnp.maximum(left_signal, right_signal)
    face_flux = 0.5 * (left_flux + right_flux) - 0.5 * signal_max * (right_state - left_state)
    return window_slice(face_flux, 1, cell_count) - window_slice(face_flux, 0, cell_count)

def tendency(padded):
    total_div = face_divergence(padded[:, :, 2:-2, 2:-2], 0)
    total_div = total_div + face_divergence(padded[:, 2:-2, :, 2:-2], 1)
    total_div = total_div + face_divergence(padded[:, 2:-2, 2:-2, :], 2)
    return -total_div

def shifted(values, direction, offset):
    for dimension in range(3):
        first_index = offset if dimension == direction else 2
        length = values.shape[dimension] - 4
        values = lax.slice_in_dim(values, first_index, first_index + length, axis=dimension)
    return values

def field_current(padded):
    magnetic = padded[4:7]

    def derivative(component, direction):
        return 0.5 * (shifted(magnetic[component], direction, 3) - shifted(magnetic[component], direction, 1))
    curl_first = derivative(2, 1) - derivative(1, 2)
    curl_second = derivative(0, 2) - derivative(2, 0)
    curl_third = derivative(1, 0) - derivative(0, 1)
    centre = [shifted(magnetic[component], 0, 2) for component in range(3)]
    field_sq = centre[0] * centre[0] + centre[1] * centre[1] + centre[2] * centre[2]
    aligned = curl_first * centre[0] + curl_second * centre[1] + curl_third * centre[2]
    return CELL_AREA * aligned / jnp.sqrt(1.0 + field_sq)

def extend(field, margin):
    field = jnp.pad(field, ((0, 0), (margin, margin), (0, 0), (0, 0)), mode='edge')
    field = jnp.pad(field, ((0, 0), (0, 0), (margin, margin), (0, 0)), mode='wrap')
    return jnp.pad(field, ((0, 0), (0, 0), (0, 0), (margin, margin)), mode='edge')

def reference(state, footpoints, conductance, inverse_blocks):
    first_padded = extend(state, 2)
    section_one = state + TIME_STEP * tendency(first_padded)
    state_next = 0.5 * state + 0.5 * (section_one + TIME_STEP * tendency(extend(section_one, 2)))
    cell_current = field_current(first_padded)
    currents = jax.ops.segment_sum(cell_current.reshape(-1), footpoints.reshape(-1), num_segments=NLAT_I * NLON_I)
    currents = currents.reshape(NLAT_I, NLON_I)

    def apply_blocks(vector):
        blocked = vector.reshape(NLAT_I, HALVES, HALF)
        result = jnp.einsum('rhij,rhj->rhi', inverse_blocks, blocked, precision=lax.Precision.HIGHEST)
        return result.reshape(NLAT_I, NLON_I)
    potential = jnp.zeros((NLAT_I, NLON_I), jnp.float32)
    for sweep_index in range(ITERS_I):
        padded_panel = jnp.pad(potential, 1)
        coupled = currents + conductance[0] * padded_panel[:-2, 1:-1]
        coupled = coupled + conductance[1] * padded_panel[2:, 1:-1]
        coupled = coupled + conductance[2] * padded_panel[1:-1, :-2]
        coupled = coupled + conductance[3] * padded_panel[1:-1, 2:]
        potential = apply_blocks(coupled)
    footpoint_potential = potential.reshape(-1)[footpoints]
    return (state_next, potential, footpoint_potential)
```

```python
import jax
import jax.numpy as jnp
from jax import lax
from jax.experimental import pallas as pl
from jax.experimental.pallas import tpu as pltpu
from jax.sharding import PartitionSpec as P

F32 = jnp.float32
BF16 = jnp.bfloat16
GAMMA = 5.0 / 3.0
TIME_STEP = 0.02
CELL_AREA = 0.125
SWEEPS = 4

NZ = 8
NXY = 16
R = 16
LON = 8
LAT = 128
FAR_FIRST_Z = (4, 3, 5, 2, 6, 1, 7)
FAR_FIRST_XY = (10, 6, 14, 2, 9, 11, 5, 7, 13, 15, 1, 3, 8, 4, 12)

NT = (((1,), (1,)), ((), ()))
MESH = pl.DeviceIdType.MESH


def minmod(a, b):
    return jnp.maximum(jnp.minimum(a, jnp.maximum(b, 0.0)), jnp.minimum(b, 0.0))


def flux(u, d):
    density, energy = u[0], u[7]
    inv = 1.0 / density
    vel = [u[1] * inv, u[2] * inv, u[3] * inv]
    mag = u[4:7]
    field_sq = mag[0] * mag[0] + mag[1] * mag[1] + mag[2] * mag[2]
    kinetic = vel[0] * vel[0] + vel[1] * vel[1] + vel[2] * vel[2]
    half_sq = 0.5 * field_sq
    pressure = (GAMMA - 1.0) * (energy - 0.5 * density * kinetic - half_sq)
    total = pressure + half_sq
    vn, bn = vel[d], mag[d]
    align = vel[0] * mag[0] + vel[1] * mag[1] + vel[2] * mag[2]
    out = [u[1 + d]]
    for k in range(3):
        m = u[1 + k] * vn - mag[k] * bn
        out.append(m + total if k == d else m)
    for k in range(3):
        out.append(None if k == d else vn * mag[k] - bn * vel[k])
    out.append((energy + total) * vn - bn * align)
    signal = jnp.abs(vn) + jnp.sqrt((GAMMA * jnp.abs(pressure) + field_sq) * inv)
    return out, signal


def face(left, right, d):
    fl, sl = flux(left, d)
    fr, sr = flux(right, d)
    top = jnp.maximum(sl, sr)
    out = []
    for k in range(8):
        jump = top * (right[k] - left[k])
        out.append(-jump if fl[k] is None else (fl[k] + fr[k]) - jump)
    return out


def split2(x):
    hi = x.astype(BF16)
    lo = (x - hi.astype(F32)).astype(BF16)
    return hi, lo


def nt(a, b):
    return lax.dot_general(a, b, NT, preferred_element_type=F32)


def lat_pass(src, base, acc):
    lane = lax.broadcasted_iota(jnp.int32, (2, LON, LAT), 2)
    last, first = lane == LAT - 1, lane == 0

    def step(i, carry):
        l = i * 2
        left, right = [], []
        for v in range(8):
            u = src[v, pl.ds(base + l, 2)]
            d = jnp.where(last, 0.0, pltpu.roll(u, LAT - 1, 2) - u)
            h = 0.5 * minmod(d, pltpu.roll(d, 1, 2))
            left.append(u + h)
            r = u - h
            right.append(jnp.where(last, r, pltpu.roll(r, LAT - 1, 2)))
        fl, sl = flux(left, 2)
        fr, sr = flux(right, 2)
        top = jnp.maximum(sl, sr)
        for v in range(8):
            jump = top * (right[v] - left[v])
            if fl[v] is None:
                f = -jump
                acc[v, pl.ds(l, 2)] = f - jnp.where(first, 0.0, pltpu.roll(f, 1, 2))
            else:
                f = (fl[v] + fr[v]) - jump
                acc[v, pl.ds(l, 2)] = f - jnp.where(first, 2.0 * fl[v], pltpu.roll(f, 1, 2))
        return carry

    lax.fori_loop(0, R // 2, step, 0)


def radial_pass(ext, acc):
    half = R // 2

    def cells(i):
        return [jnp.stack([ext[v, i], ext[v, i + half]]) for v in range(8)]

    def advance(f, prev, here):
        nxt = cells(f + 2)
        left, right, jumps = [], [], []
        for v in range(8):
            d = nxt[v] - here[v]
            h = 0.5 * minmod(d, prev[v])
            jumps.append(d)
            left.append(here[v] + h)
            right.append(here[v] - h)
        return nxt, jumps, left, right

    c0, c1 = cells(0), cells(1)
    prev = [c1[v] - c0[v] for v in range(8)]
    here, prev, left, _ = advance(0, prev, c1)
    here, prev, left2, right = advance(1, prev, here)
    f0 = face(left, right, 0)

    def step(i, carry):
        here, prev, left, f0 = carry
        here, prev, left2, right = advance(i + 2, prev, here)
        f1 = face(left, right, 0)
        for v in range(8):
            df = f1[v] - f0[v]
            acc[v, i] += df[0]
            acc[v, i + half] += df[1]
        return here, prev, left2, f1

    lax.fori_loop(0, half, step, (here, prev, left2, f0))


def lon_pass(ext, acc):
    def advance(i, prev, here):
        left, right, jumps, nxt = [], [], [], []
        for v in range(8):
            n = ext[v, i]
            d = n - here[v]
            h = 0.5 * minmod(d, prev[v])
            nxt.append(n)
            jumps.append(d)
            left.append(here[v] + h)
            right.append(here[v] - h)
        return nxt, jumps, left, right

    c0 = [ext[v, 0] for v in range(8)]
    c1 = [ext[v, 1] for v in range(8)]
    prev = [c1[v] - c0[v] for v in range(8)]
    here, prev, left, _ = advance(2, prev, c1)
    here, prev, left2, right = advance(3, prev, here)
    f0 = face(left, right, 1)

    def step(i, carry):
        here, prev, left, f0 = carry
        here, prev, left2, right = advance(i + 4, prev, here)
        f1 = face(left, right, 1)
        for v in range(8):
            acc[v, i] = f1[v] - f0[v]
        return here, prev, left2, f1

    lax.fori_loop(0, LON, step, (here, prev, left2, f0))


def kernel(
    state, foot, cond, inv,
    out_state, out_pot, out_foot,
    xr, xt, yr, yt, acc, acct, dt1,
    part, zb, zs, ab, prow, sweep, zp, ps, ap,
    send_sem, recv_sem,
):
    s = lax.axis_index("shell")
    h = lax.axis_index("radial")
    z, xy = s % NZ, s // NZ
    base = s - z
    right = ((s + 1) % (NZ * NXY), h)
    left = ((s + NZ * NXY - 1) % (NZ * NXY), h)
    mate = (s, 1 - h)
    line = [(base + (z + k) % NZ, c) for k in FAR_FIRST_Z for c in (0, 1)] + [mate]
    plane = [((xy + k) % NXY * NZ + z, h) for k in FAR_FIRST_XY]
    slot = z * 2 + h

    def remote(src, dst, n, device):
        copy = pltpu.make_async_remote_copy(
            src_ref=src, dst_ref=dst, send_sem=send_sem.at[n], recv_sem=recv_sem.at[n],
            device_id=device, device_id_type=MESH,
        )
        copy.start()
        return copy

    def landed(ref, n):
        pltpu.make_async_copy(ref, ref, recv_sem.at[n]).wait()

    def sent(ref, n):
        pltpu.make_async_copy(ref, ref, send_sem.at[n]).wait()

    barrier = pltpu.get_barrier_semaphore()
    partners = line + plane + [right, left]
    for device in partners:
        pl.semaphore_signal(barrier, inc=1, device_id=device, device_id_type=MESH)

    for v in (4, 5, 6, 0, 1, 2, 3, 7):
        for j in range(LON):
            xt[v, j + 2] = state[v, :, j, :]
    edge, low = 18 * h, 14 * (1 - h)
    for v in range(8):
        xr[v, pl.ds(2, R)] = state[v]
        e = state[v, 15 * h]
        xr[v, edge] = e
        xr[v, edge + 1] = e
    inv_hi, inv_lo = split2(inv[0, 0])
    pl.semaphore_wait(barrier, len(partners))

    copies = []
    for n, lo, cnt in ((0, 4, 3), (3, 0, 4), (6, 7, 1)):
        vs = pl.ds(lo, cnt)
        copies.append(remote(state.at[vs, pl.ds(low, 2)], xr.at[vs, pl.ds(edge, 2)], n, mate))
        copies.append(remote(xt.at[vs, pl.ds(8, 2)], xt.at[vs, pl.ds(0, 2)], n + 1, right))
        copies.append(remote(xt.at[vs, pl.ds(2, 2)], xt.at[vs, pl.ds(10, 2)], n + 2, left))

    lat_pass(state, 0, acc)

    for c in copies[:3]:
        c.wait_recv()
    for k, v in enumerate((6, 4)):
        for j in range(LON):
            dt1[k, j] = xt[v, j + 3] - xt[v, j + 1]
    lane3 = lax.broadcasted_iota(jnp.int32, (LON, LAT), 1)
    first, last = lane3 == 0, lane3 == LAT - 1
    row16 = lax.broadcasted_iota(jnp.int32, (16, LAT), 0)

    def along_lat(b):
        up = jnp.where(last, b, pltpu.roll(b, LAT - 1, 1))
        down = jnp.where(first, b, pltpu.roll(b, 1, 1))
        return up - down

    def current_step(l, total):
        b = [xr[v, l + 2] for v in (4, 5, 6)]
        up = [xr[v, l + 3] for v in (5, 6)]
        dn = [xr[v, l + 1] for v in (5, 6)]
        c0 = dt1[0, :, l, :] - along_lat(b[1])
        c1 = along_lat(b[0]) - (up[1] - dn[1])
        c2 = (up[0] - dn[0]) - dt1[1, :, l, :]
        sq = b[0] * b[0] + b[1] * b[1] + b[2] * b[2]
        val = (0.5 * CELL_AREA) * (c0 * b[0] + c1 * b[1] + c2 * b[2]) / jnp.sqrt(1.0 + sq)
        hi = val.astype(BF16).astype(F32)
        lo = (val - hi).astype(BF16).astype(F32)
        node = foot[l]
        row = jnp.right_shift(node, 8)
        group = jnp.bitwise_and(node, 1) * 8 + jnp.right_shift(row, 4)
        inner = jnp.bitwise_and(row, 15)
        a, bmat = [], []
        for j in range(LON):
            hit = jnp.broadcast_to(group[j : j + 1], (16, LAT)) == row16
            a.append(
                jnp.concatenate(
                    [
                        jnp.where(hit, jnp.broadcast_to(hi[j : j + 1], (16, LAT)), 0.0).astype(BF16),
                        jnp.where(hit, jnp.broadcast_to(lo[j : j + 1], (16, LAT)), 0.0).astype(BF16),
                    ],
                    axis=0,
                )
            )
            one = jnp.where(jnp.broadcast_to(inner[j : j + 1], (16, LAT)) == row16, 1.0, 0.0)
            bmat.append(jnp.concatenate([one.astype(BF16)] * 8, axis=0))
        return total + nt(jnp.concatenate(a, axis=1), jnp.concatenate(bmat, axis=1))

    total = lax.fori_loop(0, R, current_step, jnp.zeros((32, LAT), F32))
    total = total[:16] + total[16:]
    lane16 = lax.broadcasted_iota(jnp.int32, (16, LAT), 1)
    total = jnp.where(jnp.right_shift(lane16, 4) == jnp.bitwise_and(row16, 7), total, 0.0)
    mine = jnp.concatenate(
        [jnp.sum(total[:8], axis=0, keepdims=True), jnp.sum(total[8:], axis=0, keepdims=True)], axis=0
    )
    part[...] = mine
    zb[slot] = mine
    for device in line:
        remote(part, zb.at[slot], 9, device)

    for c in copies[3:]:
        c.wait_recv()
    radial_pass(xr, acc)

    landed(zb.at[pl.ds(0, 15)], 9)
    for k in range(NZ):
        zs[2 * k : 2 * k + 2, :] = zb[2 * k] + zb[2 * k + 1]
    ab[xy] = zs[...]
    for device in plane:
        remote(zs, ab.at[xy], 10, device)

    lon_pass(xt, acct)

    def section_one(l, carry):
        for v in range(8):
            yr[v, l + 2] = state[v, l] - (0.5 * TIME_STEP) * (acc[v, l] + acct[v, :, l, :])
        return carry

    lax.fori_loop(0, R, section_one, 0)
    for v in range(8):
        for j in range(LON):
            yt[v, j + 2] = yr[v, 2 : R + 2, j, :]
        e = yr[v, 2 + 15 * h]
        yr[v, edge] = e
        yr[v, edge + 1] = e
    again = [
        remote(yr.at[:, pl.ds(2 + low, 2)], yr.at[:, pl.ds(edge, 2)], 11, mate),
        remote(yt.at[:, pl.ds(8, 2)], yt.at[:, pl.ds(0, 2)], 12, right),
        remote(yt.at[:, pl.ds(2, 2)], yt.at[:, pl.ds(10, 2)], 13, left),
    ]

    landed(ab.at[pl.ds(0, 15)], 10)
    lane8 = lax.broadcasted_iota(jnp.int32, (16, LAT), 1)
    pick = jnp.where(lane8 == s, 1.0, 0.0).astype(BF16)
    mine_hi, mine_lo = split2(ab[pl.ds(8 * h, 8)].reshape(LAT, LAT))
    currents = (nt(pick, mine_hi) + nt(pick, mine_lo))[:8]

    def apply_block(vector):
        hi, lo = split2(vector)
        both = nt(jnp.concatenate([hi, lo], axis=0), inv_hi)
        return both[:8] + both[8:] + nt(jnp.concatenate([hi, lo], axis=0), inv_lo)[:8]

    lane_1 = lax.broadcasted_iota(jnp.int32, (8, LAT), 1)
    col_first, col_last = lane_1 == 0, lane_1 == LAT - 1
    keep_n = jnp.where(s > 0, 1.0, 0.0).astype(F32)
    keep_s = jnp.where(s < NZ * NXY - 1, 1.0, 0.0).astype(F32)
    keep_w = h.astype(F32)
    keep_e = (1 - h).astype(F32)

    potential = apply_block(currents)
    hops = []
    for k in range(SWEEPS - 1):
        prow[k] = potential[:1]
        trio = [
            remote(prow.at[k], sweep.at[3 * k], 14 + 3 * k, right),
            remote(prow.at[k], sweep.at[3 * k + 1], 15 + 3 * k, left),
            remote(prow.at[k], sweep.at[3 * k + 2], 16 + 3 * k, mate),
        ]
        hops += trio
        if k == 0:
            lat_pass(yr, 2, acc)
        if k == 1:
            for c in again:
                c.wait_recv()
            radial_pass(yr, acc)
        for c in trio:
            c.wait_recv()
        north = jnp.broadcast_to(sweep[3 * k], (8, LAT)) * keep_n
        south = jnp.broadcast_to(sweep[3 * k + 1], (8, LAT)) * keep_s
        other = jnp.broadcast_to(sweep[3 * k + 2], (8, LAT))
        west = jnp.where(col_first, pltpu.roll(other, 1, 1) * keep_w, pltpu.roll(potential, 1, 1))
        east = jnp.where(col_last, pltpu.roll(other, LAT - 1, 1) * keep_e, pltpu.roll(potential, LAT - 1, 1))
        coupled = currents + cond[0] * north + cond[1] * south + cond[2] * west + cond[3] * east
        potential = apply_block(coupled)

    out_pot[...] = potential[:1]
    prow[SWEEPS - 1] = potential[:1]
    zp[slot] = potential[:1]
    for device in line:
        remote(prow.at[SWEEPS - 1], zp.at[slot], 23, device)

    lon_pass(yt, acct)

    landed(zp.at[pl.ds(0, 15)], 23)
    ps[...] = jnp.concatenate(
        [jnp.concatenate([zp[2 * k], zp[2 * k + 1]], axis=1) for k in range(NZ)], axis=0
    )
    ap[xy] = ps[...]
    for device in plane:
        remote(ps, ap.at[xy], 24, device)

    def last_step(l, carry):
        for v in range(8):
            out_state[v, l] = 0.5 * (
                state[v, l] + yr[v, l + 2] - (0.5 * TIME_STEP) * (acc[v, l] + acct[v, :, l, :])
            )
        return carry

    lax.fori_loop(0, R, last_step, 0)

    landed(ap.at[pl.ds(0, 15)], 24)
    lane256 = lax.broadcasted_iota(jnp.int32, (16, 2 * LAT), 1)
    sub256 = lax.broadcasted_iota(jnp.int32, (16, 2 * LAT), 0)
    pick2 = jnp.where(lane256 == 2 * s + sub256, 1.0, 0.0).astype(BF16)
    hi, lo = split2(ap[...].reshape(LAT, 2 * LAT))
    table = nt(pick2, hi) + nt(pick2, lo)
    tab0 = jnp.broadcast_to(table[0:1], (LON, LAT))
    tab1 = jnp.broadcast_to(table[1:2], (LON, LAT))

    def gather_step(l, carry):
        node = foot[l]
        row = jnp.right_shift(node, 8)
        even = jnp.bitwise_and(node, 1) == 0
        out_foot[l] = jnp.where(
            even,
            jnp.take_along_axis(tab0, row, axis=1, mode="promise_in_bounds"),
            jnp.take_along_axis(tab1, row, axis=1, mode="promise_in_bounds"),
        )
        return carry

    lax.fori_loop(0, R, gather_step, 0)

    for c in copies + again + hops:
        c.wait_send()
    sent(zb.at[pl.ds(0, 15)], 9)
    sent(ab.at[pl.ds(0, 15)], 10)
    sent(zp.at[pl.ds(0, 15)], 23)
    sent(ap.at[pl.ds(0, 15)], 24)


def body(state, footpoints, conductance, inverse_blocks):
    vmem = pl.BlockSpec(memory_space=pltpu.VMEM)
    return pl.pallas_call(
        kernel,
        out_shape=(
            jax.ShapeDtypeStruct((8, R, LON, LAT), F32),
            jax.ShapeDtypeStruct((1, LAT), F32),
            jax.ShapeDtypeStruct((R, LON, LAT), F32),
        ),
        in_specs=[vmem] * 4,
        out_specs=(vmem, vmem, vmem),
        scratch_shapes=[
            pltpu.VMEM((8, R + 4, LON, LAT), F32),
            pltpu.VMEM((8, LON + 4, R, LAT), F32),
            pltpu.VMEM((8, R + 4, LON, LAT), F32),
            pltpu.VMEM((8, LON + 4, R, LAT), F32),
            pltpu.VMEM((8, R, LON, LAT), F32),
            pltpu.VMEM((8, LON, R, LAT), F32),
            pltpu.VMEM((2, LON, R, LAT), F32),
            pltpu.VMEM((2, LAT), F32),
            pltpu.VMEM((16, 2, LAT), F32),
            pltpu.VMEM((16, LAT), F32),
            pltpu.VMEM((NXY, 16, LAT), F32),
            pltpu.VMEM((SWEEPS, 1, LAT), F32),
            pltpu.VMEM((9, 1, LAT), F32),
            pltpu.VMEM((16, 1, LAT), F32),
            pltpu.VMEM((NZ, 2 * LAT), F32),
            pltpu.VMEM((NXY, NZ, 2 * LAT), F32),
            pltpu.SemaphoreType.DMA((25,)),
            pltpu.SemaphoreType.DMA((25,)),
        ],
        compiler_params=pltpu.CompilerParams(
            collective_id=0, has_side_effects=True, vmem_limit_bytes=40 << 20
        ),
    )(state, footpoints, conductance, inverse_blocks)


def solution(mesh):
    return jax.shard_map(
        body,
        mesh=mesh,
        in_specs=(
            P(None, "radial", "shell", None),
            P("radial", "shell", None),
            P(None, "shell", "radial"),
            P("shell", "radial", None, None),
        ),
        out_specs=(
            P(None, "radial", "shell", None),
            P("shell", "radial"),
            P("radial", "shell", None),
        ),
        check_vma=False,
    )
```

```python
import jax
import jax.numpy as jnp
from jax import lax
from jax.experimental import pallas as pl
from jax.experimental.pallas import tpu as pltpu
from jax.sharding import PartitionSpec as P

F32 = jnp.float32
BF16 = jnp.bfloat16
GAMMA = 5.0 / 3.0
TIME_STEP = 0.02
CELL_AREA = 0.125
REACH = 3

NZ = 8
NXY = 16
R = 16
LON = 8
LAT = 128
FAR_FIRST_Z = (4, 3, 5, 2, 6, 1, 7)
FAR_FIRST_XY = (10, 6, 14, 2, 9, 11, 5, 7, 13, 15, 1, 3, 8, 4, 12)

NT = (((1,), (1,)), ((), ()))
MESH = pl.DeviceIdType.MESH


def minmod(a, b):
    return jnp.maximum(jnp.minimum(a, jnp.maximum(b, 0.0)), jnp.minimum(b, 0.0))


def flux(u, d):
    density, energy = u[0], u[7]
    inv = 1.0 / density
    vel = [u[1] * inv, u[2] * inv, u[3] * inv]
    mag = u[4:7]
    field_sq = mag[0] * mag[0] + mag[1] * mag[1] + mag[2] * mag[2]
    kinetic = vel[0] * vel[0] + vel[1] * vel[1] + vel[2] * vel[2]
    half_sq = 0.5 * field_sq
    pressure = (GAMMA - 1.0) * (energy - 0.5 * density * kinetic - half_sq)
    total = pressure + half_sq
    vn, bn = vel[d], mag[d]
    align = vel[0] * mag[0] + vel[1] * mag[1] + vel[2] * mag[2]
    out = [u[1 + d]]
    for k in range(3):
        m = u[1 + k] * vn - mag[k] * bn
        out.append(m + total if k == d else m)
    for k in range(3):
        out.append(None if k == d else vn * mag[k] - bn * vel[k])
    out.append((energy + total) * vn - bn * align)
    signal = jnp.abs(vn) + jnp.sqrt((GAMMA * jnp.abs(pressure) + field_sq) * inv)
    return out, signal


def face(left, right, d):
    fl, sl = flux(left, d)
    fr, sr = flux(right, d)
    top = jnp.maximum(sl, sr)
    out = []
    for k in range(8):
        jump = top * (right[k] - left[k])
        out.append(-jump if fl[k] is None else (fl[k] + fr[k]) - jump)
    return out


def split2(x):
    hi = x.astype(BF16)
    lo = (x - hi.astype(F32)).astype(BF16)
    return hi, lo


def nt(a, b):
    return lax.dot_general(a, b, NT, preferred_element_type=F32)


def lat_pass(src, base, acc):
    lane = lax.broadcasted_iota(jnp.int32, (2, LON, LAT), 2)
    last, first = lane == LAT - 1, lane == 0

    def step(i, carry):
        l = i * 2
        left, right = [], []
        for v in range(8):
            u = src[v, pl.ds(base + l, 2)]
            d = jnp.where(last, 0.0, pltpu.roll(u, LAT - 1, 2) - u)
            h = 0.5 * minmod(d, pltpu.roll(d, 1, 2))
            left.append(u + h)
            r = u - h
            right.append(jnp.where(last, r, pltpu.roll(r, LAT - 1, 2)))
        fl, sl = flux(left, 2)
        fr, sr = flux(right, 2)
        top = jnp.maximum(sl, sr)
        for v in range(8):
            jump = top * (right[v] - left[v])
            if fl[v] is None:
                f = -jump
                acc[v, pl.ds(l, 2)] = f - jnp.where(first, 0.0, pltpu.roll(f, 1, 2))
            else:
                f = (fl[v] + fr[v]) - jump
                acc[v, pl.ds(l, 2)] = f - jnp.where(first, 2.0 * fl[v], pltpu.roll(f, 1, 2))
        return carry

    lax.fori_loop(0, R // 2, step, 0)


def radial_pass(ext, acc):
    half = R // 2

    def cells(i):
        return [jnp.stack([ext[v, i], ext[v, i + half]]) for v in range(8)]

    def advance(f, prev, here):
        nxt = cells(f + 2)
        left, right, jumps = [], [], []
        for v in range(8):
            d = nxt[v] - here[v]
            h = 0.5 * minmod(d, prev[v])
            jumps.append(d)
            left.append(here[v] + h)
            right.append(here[v] - h)
        return nxt, jumps, left, right

    c0, c1 = cells(0), cells(1)
    prev = [c1[v] - c0[v] for v in range(8)]
    here, prev, left, _ = advance(0, prev, c1)
    here, prev, left2, right = advance(1, prev, here)
    f0 = face(left, right, 0)

    def step(i, carry):
        here, prev, left, f0 = carry
        here, prev, left2, right = advance(i + 2, prev, here)
        f1 = face(left, right, 0)
        for v in range(8):
            df = f1[v] - f0[v]
            acc[v, i] += df[0]
            acc[v, i + half] += df[1]
        return here, prev, left2, f1

    lax.fori_loop(0, half, step, (here, prev, left2, f0))


def lon_pass(ext, acc):
    def advance(i, prev, here):
        left, right, jumps, nxt = [], [], [], []
        for v in range(8):
            n = ext[v, i]
            d = n - here[v]
            h = 0.5 * minmod(d, prev[v])
            nxt.append(n)
            jumps.append(d)
            left.append(here[v] + h)
            right.append(here[v] - h)
        return nxt, jumps, left, right

    c0 = [ext[v, 0] for v in range(8)]
    c1 = [ext[v, 1] for v in range(8)]
    prev = [c1[v] - c0[v] for v in range(8)]
    here, prev, left, _ = advance(2, prev, c1)
    here, prev, left2, right = advance(3, prev, here)
    f0 = face(left, right, 1)

    def step(i, carry):
        here, prev, left, f0 = carry
        here, prev, left2, right = advance(i + 4, prev, here)
        f1 = face(left, right, 1)
        for v in range(8):
            acc[v, i] = f1[v] - f0[v]
        return here, prev, left2, f1

    lax.fori_loop(0, LON, step, (here, prev, left2, f0))


def kernel(
    state, foot_hbm, cond, inv,
    out_state, out_pot, out_table,
    foot, xr, xt, yr, yt, acc, acct, dt1, edge_in,
    part, zb, a1s, a1, prow, zp, a2s, a2,
    blocks, conds, qa, qb, green, kk,
    send_sem, recv_sem, local_sem,
):
    s = lax.axis_index("shell")
    h = lax.axis_index("radial")
    ring = NZ * NXY
    z, xy = s % NZ, s // NZ
    base = s - z
    right = ((s + 1) % ring, h)
    left = ((s + ring - 1) % ring, h)
    mate = (s, 1 - h)
    line = [(base + (z + k) % NZ, c) for k in FAR_FIRST_Z for c in (0, 1)] + [mate]
    plane = [((xy + k) % NXY, ((xy + k) % NXY * NZ + z, h)) for k in FAR_FIRST_XY]
    slot = z * 2 + h
    count = [0]

    def fresh():
        count[0] += 1
        return count[0] - 1

    def remote(src, dst, device, n=None):
        n = fresh() if n is None else n
        copy = pltpu.make_async_remote_copy(
            src_ref=src, dst_ref=dst, send_sem=send_sem.at[n], recv_sem=recv_sem.at[n],
            device_id=device, device_id_type=MESH,
        )
        copy.start()
        return copy

    def landed(ref, n):
        pltpu.make_async_copy(ref, ref, recv_sem.at[n]).wait()

    def sent(ref, n):
        pltpu.make_async_copy(ref, ref, send_sem.at[n]).wait()

    barrier = pltpu.get_barrier_semaphore()
    partners = line + [p for _, p in plane] + [right, left]
    for device in partners:
        pl.semaphore_signal(barrier, inc=1, device_id=device, device_id_type=MESH)

    inner = pl.ds(2, R)
    loads = [
        pltpu.make_async_copy(state.at[pl.ds(4, 3)], xr.at[pl.ds(4, 3), inner], local_sem.at[0]),
        pltpu.make_async_copy(state.at[pl.ds(0, 4)], xr.at[pl.ds(0, 4), inner], local_sem.at[1]),
        pltpu.make_async_copy(state.at[pl.ds(7, 1)], xr.at[pl.ds(7, 1), inner], local_sem.at[2]),
        pltpu.make_async_copy(foot_hbm, foot, local_sem.at[3]),
        pltpu.make_async_copy(inv.at[0, 0], blocks.at[3, 0], local_sem.at[4]),
        pltpu.make_async_copy(cond, conds.at[3, 0], local_sem.at[5]),
    ]
    for c in loads:
        c.start()

    def turn(dst, src, v):
        for j in range(LON):
            dst[v, j + 2] = src[v, 2 : R + 2, j, :]

    loads[0].wait()
    for v in (4, 6):
        turn(xt, xr, v)
    pl.semaphore_wait(barrier, len(partners))

    edge, low = 18 * h, 14 * (1 - h)
    copies, near = [], []
    for k, v in enumerate((6, 4)):
        near.append(remote(xt.at[v, 9], edge_in.at[k, 0], right))
        near.append(remote(xt.at[v, 2], edge_in.at[k, 1], left))
    near.append(remote(state.at[pl.ds(4, 3), pl.ds(low, 2)], xr.at[pl.ds(4, 3), pl.ds(edge, 2)], mate))

    own_block, own_cond = inv.at[0, 0], cond
    go_right = [remote(own_cond, conds.at[2, 0], right), remote(own_block, blocks.at[2, 0], right)]
    go_left = [remote(own_cond, conds.at[4, 0], left), remote(own_block, blocks.at[4, 0], left)]
    go_mate = [remote(own_cond, conds.at[3, 1], mate), remote(own_block, blocks.at[3, 1], mate)]
    side = [
        remote(state.at[pl.ds(0, 4), pl.ds(low, 2)], xr.at[pl.ds(0, 4), pl.ds(edge, 2)], mate),
        remote(state.at[pl.ds(7, 1), pl.ds(low, 2)], xr.at[pl.ds(7, 1), pl.ds(edge, 2)], mate),
    ]

    loads[1].wait()
    loads[2].wait()
    for v in (5, 0, 1, 2, 3, 7):
        turn(xt, xr, v)
    for v in range(8):
        e = xr[v, 2 + 15 * h]
        xr[v, edge] = e
        xr[v, edge + 1] = e
    lat_pass(xr, 2, acc)

    loads[3].wait()
    for c in near:
        c.wait_recv()
    for k, v in enumerate((6, 4)):
        dt1[k, 0] = xt[v, 3] - edge_in[k, 0]
        for j in range(1, LON - 1):
            dt1[k, j] = xt[v, j + 3] - xt[v, j + 1]
        dt1[k, LON - 1] = edge_in[k, 1] - xt[v, LON]
    lane = lax.broadcasted_iota(jnp.int32, (LON, LAT), 1)
    first, last = lane == 0, lane == LAT - 1
    row16 = lax.broadcasted_iota(jnp.int32, (16, LAT), 0)
    lane16 = lax.broadcasted_iota(jnp.int32, (16, LAT), 1)

    def along_lat(b):
        up = jnp.where(last, b, pltpu.roll(b, LAT - 1, 1))
        down = jnp.where(first, b, pltpu.roll(b, 1, 1))
        return up - down

    def current_step(i, total):
        a, ones = [], []
        for t in range(4):
            l = i * 4 + t
            b = [xr[v, l + 2] for v in (4, 5, 6)]
            up = [xr[v, l + 3] for v in (5, 6)]
            dn = [xr[v, l + 1] for v in (5, 6)]
            c0 = dt1[0, :, l, :] - along_lat(b[1])
            c1 = along_lat(b[0]) - (up[1] - dn[1])
            c2 = (up[0] - dn[0]) - dt1[1, :, l, :]
            sq = b[0] * b[0] + b[1] * b[1] + b[2] * b[2]
            val = (0.5 * CELL_AREA) * (c0 * b[0] + c1 * b[1] + c2 * b[2]) / jnp.sqrt(1.0 + sq)
            hi = val.astype(BF16).astype(F32)
            lo = val - hi
            node = foot[l]
            row = jnp.right_shift(node, 8)
            group = jnp.bitwise_and(node, 1) * 8 + jnp.right_shift(row, 4)
            within = jnp.bitwise_and(row, 15)
            for j in range(LON):
                hit = jnp.broadcast_to(group[j : j + 1], (16, LAT)) == row16
                top = jnp.where(hit, jnp.broadcast_to(hi[j : j + 1], (16, LAT)), 0.0)
                low_part = jnp.where(hit, jnp.broadcast_to(lo[j : j + 1], (16, LAT)), 0.0)
                a.append(jnp.concatenate([top.astype(BF16), low_part.astype(BF16)], axis=0))
                one = jnp.where(jnp.broadcast_to(within[j : j + 1], (16, LAT)) == row16, 1.0, 0.0)
                ones.append(one.astype(BF16))
        return total + nt(jnp.concatenate(a, axis=1), jnp.concatenate(ones, axis=1))

    total = lax.fori_loop(0, R // 4, current_step, jnp.zeros((32, 16), F32))
    spread = jnp.where(jnp.bitwise_and(lane16, 15) == row16, 1.0, 0.0).astype(BF16)
    t_hi, t_lo = split2(total[:16] + total[16:])
    total = jnp.dot(jnp.concatenate([t_hi, t_lo], axis=0), spread, preferred_element_type=F32)
    total = jnp.where(
        jnp.right_shift(lane16, 4) == jnp.bitwise_and(row16, 7), total[:16] + total[16:], 0.0
    )
    mine = jnp.concatenate(
        [jnp.sum(total[:8], axis=0, keepdims=True), jnp.sum(total[8:], axis=0, keepdims=True)], axis=0
    )
    part[...] = mine
    zb[slot] = mine
    n_zb = fresh()
    for device in line:
        remote(part, zb.at[slot], device, n_zb)

    copies += [
        remote(xt.at[:, pl.ds(8, 2)], xt.at[:, pl.ds(0, 2)], right),
        remote(xt.at[:, pl.ds(2, 2)], xt.at[:, pl.ds(10, 2)], left),
    ]
    for c in go_right + go_left + go_mate + side:
        c.wait_recv()
    hop_right = [remote(conds.at[2, 0], conds.at[1, 0], right), remote(blocks.at[2, 0], blocks.at[1, 0], right)]
    hop_left = [remote(conds.at[4, 0], conds.at[5, 0], left), remote(blocks.at[4, 0], blocks.at[5, 0], left)]
    hop_mate = [
        remote(conds.at[2, 0], conds.at[2, 1], mate), remote(blocks.at[2, 0], blocks.at[2, 1], mate),
        remote(conds.at[4, 0], conds.at[4, 1], mate), remote(blocks.at[4, 0], blocks.at[4, 1], mate),
    ]
    loads[4].wait()
    loads[5].wait()

    lane32 = lax.broadcasted_iota(jnp.int32, (32, LAT), 1)
    low32, high32 = lane32 == 0, lane32 == LAT - 1
    is_low = ((1 - h).astype(F32), h.astype(F32))
    is_high = (h.astype(F32), (1 - h).astype(F32))

    def north(d, c):
        return conds[d + 3, c, 0] * jnp.where(s + d == 0, 0.0, 1.0)

    def south(d, c):
        return conds[d + 3, c, 1] * jnp.where(s + d == ring - 1, 0.0, 1.0)

    def widen(source, target, level):
        there = lambda d, c: abs(d) <= level - c
        for c in (0, 1):
            for d in range(c - level - 1, level + 2 - c):
                for i in range(0, LAT, 32):
                    rows = pl.ds(i, 32)
                    terms = []
                    if there(d + 1, c):
                        terms.append(source(d + 1, c)[rows] * north(d + 1, c))
                    if there(d - 1, c):
                        terms.append(source(d - 1, c)[rows] * south(d - 1, c))
                    w, e = None, None
                    if there(d, c):
                        me = source(d, c)[rows]
                        w, e = me * conds[d + 3, c, 2], me * conds[d + 3, c, 3]
                    if there(d, 1 - c):
                        ot = source(d, 1 - c)[rows]
                        zero = jnp.zeros_like(ot)
                        w = jnp.where(low32, ot * (conds[d + 3, 1 - c, 2] * is_low[c]), zero if w is None else w)
                        e = jnp.where(high32, ot * (conds[d + 3, 1 - c, 3] * is_high[c]), zero if e is None else e)
                    elif w is not None:
                        w, e = jnp.where(low32, 0.0, w), jnp.where(high32, 0.0, e)
                    if w is not None:
                        terms += [pltpu.roll(w, LAT - 1, 1), pltpu.roll(e, 1, 1)]
                    k_hi, k_lo = split2(sum(terms[1:], terms[0]))
                    kk[rows, :] = jnp.concatenate([k_hi, k_hi, k_lo], axis=1)
                b_hi, b_lo = split2(blocks[d + 3, c])
                q = jnp.dot(kk[...], jnp.concatenate([b_hi, b_lo, b_hi], axis=0), preferred_element_type=F32)
                if target is not None:
                    target[d + 3, c] = q
                if there(d, c):
                    green[d + 3, c] += q
                else:
                    green[d + 3, c] = q

    green[3, 0] = blocks[3, 0]
    widen(lambda d, c: blocks.at[d + 3, c], qb, 0)
    radial_pass(xr, acc)

    landed(zb.at[pl.ds(0, 15)], n_zb)
    columns = jnp.concatenate([zb[2 * k] + zb[2 * k + 1] for k in range(NZ)], axis=0)
    row128 = lax.broadcasted_iota(jnp.int32, (LAT, LAT), 0)
    lane128 = lax.broadcasted_iota(jnp.int32, (LAT, LAT), 1)
    placed = jnp.where(
        jnp.right_shift(row128, 4) == xy % 8, jnp.concatenate([columns] * 8, axis=0), 0.0
    )
    pick = jnp.where(lane128 == row128 + (z - REACH), 1.0, 0.0).astype(BF16)
    p_hi, p_lo = split2(placed)
    a1s[...] = (nt(pick, p_hi) + nt(pick, p_lo)).reshape(NXY, 8, LAT)
    n_a1 = fresh()
    for to, device in plane:
        remote(a1s.at[to], a1.at[xy], device, n_a1)
    a1[xy] = a1s[xy]

    for c in hop_right + hop_left + hop_mate:
        c.wait_recv()
    end_right = [remote(blocks.at[1, 0], blocks.at[0, 0], right)]
    end_left = [remote(blocks.at[5, 0], blocks.at[6, 0], left)]
    end_mate = [remote(blocks.at[1, 0], blocks.at[1, 1], mate), remote(blocks.at[5, 0], blocks.at[5, 1], mate)]
    widen(lambda d, c: qb.at[d + 3, c], qa, 1)
    for c in copies:
        c.wait_recv()
    lon_pass(xt, acct)

    def section_one(l, carry):
        for v in range(8):
            yr[v, l + 2] = xr[v, l + 2] - (0.5 * TIME_STEP) * (acc[v, l] + acct[v, :, l, :])
        return carry

    lax.fori_loop(0, R, section_one, 0)
    for v in range(8):
        turn(yt, yr, v)
        e = yr[v, 2 + 15 * h]
        yr[v, edge] = e
        yr[v, edge + 1] = e
    for c in end_right + end_left + end_mate:
        c.wait_recv()
    widen(lambda d, c: qa.at[d + 3, c], None, 2)

    landed(a1.at[pl.ds(0, 15)], n_a1)
    out = jnp.zeros((LAT, LAT), F32)
    for c in (0, 1):
        first_source = 8 * h if c == 0 else 8 * (1 - h)
        rows = a1[first_source]
        for k in range(1, 8):
            rows = rows + a1[first_source + k]
        for d in range(c - REACH, REACH + 1 - c):
            out = out + green[d + 3, c] * jnp.broadcast_to(rows[d + 3 : d + 4], (LAT, LAT))
    o_hi, o_lo = split2(out)
    all_ones = jnp.ones((16, LAT), BF16)
    potential = (nt(all_ones, o_hi) + nt(all_ones, o_lo))[:1]
    out_pot[...] = potential
    prow[...] = potential
    zp[slot] = potential
    n_zp = fresh()
    for device in line:
        remote(prow, zp.at[slot], device, n_zp)

    again = [
        remote(yr.at[:, pl.ds(2 + low, 2)], yr.at[:, pl.ds(edge, 2)], mate),
        remote(yt.at[:, pl.ds(8, 2)], yt.at[:, pl.ds(0, 2)], right),
        remote(yt.at[:, pl.ds(2, 2)], yt.at[:, pl.ds(10, 2)], left),
    ]
    lat_pass(yr, 2, acc)

    landed(zp.at[pl.ds(0, 15)], n_zp)
    lines = jnp.concatenate(
        [jnp.concatenate([zp[2 * k], zp[2 * k + 1]], axis=1) for k in range(NZ)], axis=0
    )
    row256 = lax.broadcasted_iota(jnp.int32, (LAT, 2 * LAT), 0)
    placed = jnp.where(jnp.right_shift(row256, 3) == xy, jnp.concatenate([lines] * NXY, axis=0), 0.0)
    m = lax.broadcasted_iota(jnp.int32, (2 * NXY, 2 * LAT), 0)
    n = lax.broadcasted_iota(jnp.int32, (2 * NXY, 2 * LAT), 1)
    pick2 = jnp.where(
        n == 2 * (jnp.right_shift(m, 1) * NZ + z) + jnp.bitwise_and(m, 1), 1.0, 0.0
    ).astype(BF16)
    l_hi, l_lo = split2(placed)
    picked = nt(pick2, l_hi) + nt(pick2, l_lo)
    for k in range(NXY):
        a2s[k] = picked[2 * k : 2 * k + 2]
    n_a2 = fresh()
    for to, device in plane:
        remote(a2s.at[to], a2.at[xy], device, n_a2)
    a2[xy] = a2s[xy]

    for c in again:
        c.wait_recv()
    radial_pass(yr, acc)
    lon_pass(yt, acct)

    def last_step(l, carry):
        for v in range(8):
            out_state[v, l] = 0.5 * (
                xr[v, l + 2] + yr[v, l + 2] - (0.5 * TIME_STEP) * (acc[v, l] + acct[v, :, l, :])
            )
        return carry

    lax.fori_loop(0, R, last_step, 0)

    landed(a2.at[pl.ds(0, 15)], n_a2)
    table = a2[0]
    for k in range(1, NXY):
        table = table + a2[k]
    out_table[...] = table

    for c in (
        near + copies + side + again + go_right + go_left + go_mate + hop_right + hop_left + hop_mate
        + end_right + end_left + end_mate
    ):
        c.wait_send()
    sent(zb.at[pl.ds(0, 15)], n_zb)
    sent(a1.at[pl.ds(0, 15)], n_a1)
    sent(zp.at[pl.ds(0, 15)], n_zp)
    sent(a2.at[pl.ds(0, 15)], n_a2)
    assert count[0] <= N_SEMS, count[0]


def finish(state, pot, table, foot, out_state, out_pot, out_foot, buf, sem):
    copies = [
        pltpu.make_async_copy(state, out_state, sem.at[0]),
        pltpu.make_async_copy(pot, out_pot, sem.at[1]),
    ]
    for c in copies:
        c.start()
    tab0 = jnp.broadcast_to(table[0:1, :], (LON, LAT))
    tab1 = jnp.broadcast_to(table[1:2, :], (LON, LAT))
    for l in range(R):
        node = foot[l]
        row = jnp.right_shift(node, 8)
        buf[l] = jnp.where(
            jnp.bitwise_and(node, 1) == 0,
            jnp.take_along_axis(tab0, row, axis=1, mode="promise_in_bounds"),
            jnp.take_along_axis(tab1, row, axis=1, mode="promise_in_bounds"),
        )
    copies.append(pltpu.make_async_copy(buf, out_foot, sem.at[2]))
    copies[2].start()
    for c in copies:
        c.wait()


N_SEMS = 48


def body(state, footpoints, conductance, inverse_blocks):
    vmem = pl.BlockSpec(memory_space=pltpu.VMEM)
    hbm = pl.BlockSpec(memory_space=pltpu.HBM)
    whole = (
        jax.ShapeDtypeStruct((8, R, LON, LAT), F32),
        jax.ShapeDtypeStruct((1, LAT), F32),
    )
    cells, potential, table = pl.pallas_call(
        kernel,
        out_shape=whole + (jax.ShapeDtypeStruct((2, LAT), F32),),
        in_specs=[hbm] * 4,
        out_specs=(vmem, vmem, vmem),
        scratch_shapes=[
            pltpu.VMEM((R, LON, LAT), jnp.int32),
            pltpu.VMEM((8, R + 4, LON, LAT), F32),
            pltpu.VMEM((8, LON + 4, R, LAT), F32),
            pltpu.VMEM((8, R + 4, LON, LAT), F32),
            pltpu.VMEM((8, LON + 4, R, LAT), F32),
            pltpu.VMEM((8, R, LON, LAT), F32),
            pltpu.VMEM((8, LON, R, LAT), F32),
            pltpu.VMEM((2, LON, R, LAT), F32),
            pltpu.VMEM((2, 2, R, LAT), F32),
            pltpu.VMEM((2, LAT), F32),
            pltpu.VMEM((16, 2, LAT), F32),
            pltpu.VMEM((NXY, 8, LAT), F32),
            pltpu.VMEM((NXY, 8, LAT), F32),
            pltpu.VMEM((1, LAT), F32),
            pltpu.VMEM((16, 1, LAT), F32),
            pltpu.VMEM((NXY, 2, LAT), F32),
            pltpu.VMEM((NXY, 2, LAT), F32),
            pltpu.VMEM((7, 2, LAT, LAT), F32),
            pltpu.VMEM((7, 2, 4, 1, LAT), F32),
            pltpu.VMEM((7, 2, LAT, LAT), F32),
            pltpu.VMEM((7, 2, LAT, LAT), F32),
            pltpu.VMEM((7, 2, LAT, LAT), F32),
            pltpu.VMEM((LAT, 3 * LAT), BF16),
            pltpu.SemaphoreType.DMA((N_SEMS,)),
            pltpu.SemaphoreType.DMA((N_SEMS,)),
            pltpu.SemaphoreType.DMA((6,)),
        ],
        compiler_params=pltpu.CompilerParams(
            collective_id=0, has_side_effects=True, vmem_limit_bytes=40 << 20
        ),
    )(state, footpoints, conductance, inverse_blocks)
    return pl.pallas_call(
        finish,
        out_shape=whole + (jax.ShapeDtypeStruct((R, LON, LAT), F32),),
        in_specs=[vmem] * 4,
        out_specs=(hbm, hbm, hbm),
        scratch_shapes=[pltpu.VMEM((R, LON, LAT), F32), pltpu.SemaphoreType.DMA((3,))],
    )(cells, potential, table, footpoints)


def solution(mesh):
    return jax.shard_map(
        body,
        mesh=mesh,
        in_specs=(
            P(None, "radial", "shell", None),
            P("radial", "shell", None),
            P(None, "shell", "radial"),
            P("shell", "radial", None, None),
        ),
        out_specs=(
            P(None, "radial", "shell", None),
            P("shell", "radial"),
            P("radial", "shell", None),
        ),
        check_vma=False,
    )
```

```python
import jax
import jax.numpy as jnp
from jax import lax
from jax.experimental import pallas as pl
from jax.experimental.pallas import tpu as pltpu
from jax.sharding import PartitionSpec as P

F32 = jnp.float32
BF16 = jnp.bfloat16
GAMMA = 5.0 / 3.0
TIME_STEP = 0.02
CELL_AREA = 0.125
REACH = 3

NZ = 8
NXY = 16
R = 16
LON = 8
LAT = 128
FAR_FIRST_Z = (4, 3, 5, 2, 6, 1, 7)
FAR_FIRST_XY = (10, 6, 14, 2, 9, 11, 5, 7, 13, 15, 1, 3, 8, 4, 12)

NT = (((1,), (1,)), ((), ()))
MESH = pl.DeviceIdType.MESH


def minmod(a, b):
    return jnp.maximum(jnp.minimum(a, jnp.maximum(b, 0.0)), jnp.minimum(b, 0.0))


def flux(u, d):
    density, energy = u[0], u[7]
    inv = 1.0 / density
    vel = [u[1] * inv, u[2] * inv, u[3] * inv]
    mag = u[4:7]
    field_sq = mag[0] * mag[0] + mag[1] * mag[1] + mag[2] * mag[2]
    kinetic = vel[0] * vel[0] + vel[1] * vel[1] + vel[2] * vel[2]
    half_sq = 0.5 * field_sq
    pressure = (GAMMA - 1.0) * (energy - 0.5 * density * kinetic - half_sq)
    total = pressure + half_sq
    vn, bn = vel[d], mag[d]
    align = vel[0] * mag[0] + vel[1] * mag[1] + vel[2] * mag[2]
    out = [u[1 + d]]
    for k in range(3):
        m = u[1 + k] * vn - mag[k] * bn
        out.append(m + total if k == d else m)
    for k in range(3):
        out.append(None if k == d else vn * mag[k] - bn * vel[k])
    out.append((energy + total) * vn - bn * align)
    signal = jnp.abs(vn) + jnp.sqrt((GAMMA * jnp.abs(pressure) + field_sq) * inv)
    return out, signal


def face(left, right, d):
    fl, sl = flux(left, d)
    fr, sr = flux(right, d)
    top = jnp.maximum(sl, sr)
    out = []
    for k in range(8):
        jump = top * (right[k] - left[k])
        out.append(-jump if fl[k] is None else (fl[k] + fr[k]) - jump)
    return out


def split2(x):
    hi = x.astype(BF16)
    lo = (x - hi.astype(F32)).astype(BF16)
    return hi, lo


def nt(a, b):
    return lax.dot_general(a, b, NT, preferred_element_type=F32)


def lat_pass(src, base, acc):
    lane = lax.broadcasted_iota(jnp.int32, (2, LON, LAT), 2)
    last, first = lane == LAT - 1, lane == 0

    def step(i, carry):
        l = i * 2
        left, right = [], []
        for v in range(8):
            u = src[v, pl.ds(base + l, 2)]
            d = jnp.where(last, 0.0, pltpu.roll(u, LAT - 1, 2) - u)
            h = 0.5 * minmod(d, pltpu.roll(d, 1, 2))
            left.append(u + h)
            r = u - h
            right.append(jnp.where(last, r, pltpu.roll(r, LAT - 1, 2)))
        fl, sl = flux(left, 2)
        fr, sr = flux(right, 2)
        top = jnp.maximum(sl, sr)
        for v in range(8):
            jump = top * (right[v] - left[v])
            if fl[v] is None:
                f = -jump
                acc[v, pl.ds(l, 2)] = f - jnp.where(first, 0.0, pltpu.roll(f, 1, 2))
            else:
                f = (fl[v] + fr[v]) - jump
                acc[v, pl.ds(l, 2)] = f - jnp.where(first, 2.0 * fl[v], pltpu.roll(f, 1, 2))
        return carry

    lax.fori_loop(0, R // 2, step, 0)


def radial_pass(ext, acc):
    half = R // 2

    def cells(i):
        return [jnp.stack([ext[v, i], ext[v, i + half]]) for v in range(8)]

    def advance(f, prev, here):
        nxt = cells(f + 2)
        left, right, jumps = [], [], []
        for v in range(8):
            d = nxt[v] - here[v]
            h = 0.5 * minmod(d, prev[v])
            jumps.append(d)
            left.append(here[v] + h)
            right.append(here[v] - h)
        return nxt, jumps, left, right

    c0, c1 = cells(0), cells(1)
    prev = [c1[v] - c0[v] for v in range(8)]
    here, prev, left, _ = advance(0, prev, c1)
    here, prev, left2, right = advance(1, prev, here)
    f0 = face(left, right, 0)

    def step(i, carry):
        here, prev, left, f0 = carry
        here, prev, left2, right = advance(i + 2, prev, here)
        f1 = face(left, right, 0)
        for v in range(8):
            df = f1[v] - f0[v]
            acc[v, i] += df[0]
            acc[v, i + half] += df[1]
        return here, prev, left2, f1

    lax.fori_loop(0, half, step, (here, prev, left2, f0))


def lon_pass(ext, acc):
    def advance(i, prev, here):
        left, right, jumps, nxt = [], [], [], []
        for v in range(8):
            n = ext[v, i]
            d = n - here[v]
            h = 0.5 * minmod(d, prev[v])
            nxt.append(n)
            jumps.append(d)
            left.append(here[v] + h)
            right.append(here[v] - h)
        return nxt, jumps, left, right

    c0 = [ext[v, 0] for v in range(8)]
    c1 = [ext[v, 1] for v in range(8)]
    prev = [c1[v] - c0[v] for v in range(8)]
    here, prev, left, _ = advance(2, prev, c1)
    here, prev, left2, right = advance(3, prev, here)
    f0 = face(left, right, 1)

    def step(i, carry):
        here, prev, left, f0 = carry
        here, prev, left2, right = advance(i + 4, prev, here)
        f1 = face(left, right, 1)
        for v in range(8):
            acc[v, i] = f1[v] - f0[v]
        return here, prev, left2, f1

    lax.fori_loop(0, LON, step, (here, prev, left2, f0))


def kernel(
    state, foot_hbm, cond, inv,
    out_state, out_pot, out_table,
    foot, xr, xt, yr, yt, acc, acct, dt1, edge_in,
    part, zb, a1s, a1, prow, zp, a2s, a2,
    blocks, conds, qa, qb, green, kk,
    send_sem, recv_sem, local_sem,
):
    s = lax.axis_index("shell")
    h = lax.axis_index("radial")
    ring = NZ * NXY
    z, xy = s % NZ, s // NZ
    base = s - z
    right = ((s + 1) % ring, h)
    left = ((s + ring - 1) % ring, h)
    mate = (s, 1 - h)
    line = [(base + (z + k) % NZ, c) for k in FAR_FIRST_Z for c in (0, 1)] + [mate]
    plane = [((xy + k) % NXY, ((xy + k) % NXY * NZ + z, h)) for k in FAR_FIRST_XY]
    slot = z * 2 + h
    count = [0]

    def fresh():
        count[0] += 1
        return count[0] - 1

    def remote(src, dst, device, n=None):
        n = fresh() if n is None else n
        copy = pltpu.make_async_remote_copy(
            src_ref=src, dst_ref=dst, send_sem=send_sem.at[n], recv_sem=recv_sem.at[n],
            device_id=device, device_id_type=MESH,
        )
        copy.start()
        return copy

    def landed(ref, n):
        pltpu.make_async_copy(ref, ref, recv_sem.at[n]).wait()

    def sent(ref, n):
        pltpu.make_async_copy(ref, ref, send_sem.at[n]).wait()

    barrier = pltpu.get_barrier_semaphore()
    partners = line + [p for _, p in plane] + [right, left]
    for device in partners:
        pl.semaphore_signal(barrier, inc=1, device_id=device, device_id_type=MESH)

    inner = pl.ds(2, R)
    loads = [
        pltpu.make_async_copy(state.at[pl.ds(4, 3)], xr.at[pl.ds(4, 3), inner], local_sem.at[0]),
        pltpu.make_async_copy(state.at[pl.ds(0, 4)], xr.at[pl.ds(0, 4), inner], local_sem.at[1]),
        pltpu.make_async_copy(state.at[pl.ds(7, 1)], xr.at[pl.ds(7, 1), inner], local_sem.at[2]),
        pltpu.make_async_copy(foot_hbm, foot, local_sem.at[3]),
        pltpu.make_async_copy(inv.at[0, 0], blocks.at[3, 0], local_sem.at[4]),
        pltpu.make_async_copy(cond, conds.at[3, 0], local_sem.at[5]),
    ]
    for c in loads:
        c.start()

    def turn(dst, src, v):
        for j in range(LON):
            dst[v, j + 2] = src[v, 2 : R + 2, j, :]

    loads[0].wait()
    for v in (4, 6):
        turn(xt, xr, v)
    pl.semaphore_wait(barrier, len(partners))

    edge, low = 18 * h, 14 * (1 - h)
    copies, near = [], []
    for k, v in enumerate((6, 4)):
        near.append(remote(xt.at[v, 9], edge_in.at[k, 0], right))
        near.append(remote(xt.at[v, 2], edge_in.at[k, 1], left))
    near.append(remote(state.at[pl.ds(4, 3), pl.ds(low, 2)], xr.at[pl.ds(4, 3), pl.ds(edge, 2)], mate))

    own_block, own_cond = inv.at[0, 0], cond
    go_right = [remote(own_cond, conds.at[2, 0], right), remote(own_block, blocks.at[2, 0], right)]
    go_left = [remote(own_cond, conds.at[4, 0], left), remote(own_block, blocks.at[4, 0], left)]
    go_mate = [remote(own_cond, conds.at[3, 1], mate), remote(own_block, blocks.at[3, 1], mate)]
    side = [
        remote(state.at[pl.ds(0, 4), pl.ds(low, 2)], xr.at[pl.ds(0, 4), pl.ds(edge, 2)], mate),
        remote(state.at[pl.ds(7, 1), pl.ds(low, 2)], xr.at[pl.ds(7, 1), pl.ds(edge, 2)], mate),
    ]

    loads[1].wait()
    loads[2].wait()
    for v in (5, 0, 1, 2, 3, 7):
        turn(xt, xr, v)
    copies += [
        remote(xt.at[:, pl.ds(8, 2)], xt.at[:, pl.ds(0, 2)], right),
        remote(xt.at[:, pl.ds(2, 2)], xt.at[:, pl.ds(10, 2)], left),
    ]
    for v in range(8):
        e = xr[v, 2 + 15 * h]
        xr[v, edge] = e
        xr[v, edge + 1] = e
    lat_pass(xr, 2, acc)

    loads[3].wait()
    for c in near:
        c.wait_recv()
    for k, v in enumerate((6, 4)):
        dt1[k, 0] = xt[v, 3] - edge_in[k, 0]
        for j in range(1, LON - 1):
            dt1[k, j] = xt[v, j + 3] - xt[v, j + 1]
        dt1[k, LON - 1] = edge_in[k, 1] - xt[v, LON]
    lane = lax.broadcasted_iota(jnp.int32, (LON, LAT), 1)
    first, last = lane == 0, lane == LAT - 1
    row16 = lax.broadcasted_iota(jnp.int32, (16, LAT), 0)
    lane16 = lax.broadcasted_iota(jnp.int32, (16, LAT), 1)

    def along_lat(b):
        up = jnp.where(last, b, pltpu.roll(b, LAT - 1, 1))
        down = jnp.where(first, b, pltpu.roll(b, 1, 1))
        return up - down

    def current_step(i, total):
        a, ones = [], []
        for t in range(4):
            l = i * 4 + t
            b = [xr[v, l + 2] for v in (4, 5, 6)]
            up = [xr[v, l + 3] for v in (5, 6)]
            dn = [xr[v, l + 1] for v in (5, 6)]
            c0 = dt1[0, :, l, :] - along_lat(b[1])
            c1 = along_lat(b[0]) - (up[1] - dn[1])
            c2 = (up[0] - dn[0]) - dt1[1, :, l, :]
            sq = b[0] * b[0] + b[1] * b[1] + b[2] * b[2]
            val = (0.5 * CELL_AREA) * (c0 * b[0] + c1 * b[1] + c2 * b[2]) / jnp.sqrt(1.0 + sq)
            hi = val.astype(BF16).astype(F32)
            lo = val - hi
            node = foot[l]
            row = jnp.right_shift(node, 8)
            group = jnp.bitwise_and(node, 1) * 8 + jnp.right_shift(row, 4)
            within = jnp.bitwise_and(row, 15)
            for j in range(LON):
                hit = jnp.broadcast_to(group[j : j + 1], (16, LAT)) == row16
                top = jnp.where(hit, jnp.broadcast_to(hi[j : j + 1], (16, LAT)), 0.0)
                low_part = jnp.where(hit, jnp.broadcast_to(lo[j : j + 1], (16, LAT)), 0.0)
                a.append(jnp.concatenate([top.astype(BF16), low_part.astype(BF16)], axis=0))
                one = jnp.where(jnp.broadcast_to(within[j : j + 1], (16, LAT)) == row16, 1.0, 0.0)
                ones.append(one.astype(BF16))
        return total + nt(jnp.concatenate(a, axis=1), jnp.concatenate(ones, axis=1))

    total = lax.fori_loop(0, R // 4, current_step, jnp.zeros((32, 16), F32))
    spread = jnp.where(jnp.bitwise_and(lane16, 15) == row16, 1.0, 0.0).astype(BF16)
    t_hi, t_lo = split2(total[:16] + total[16:])
    total = jnp.dot(jnp.concatenate([t_hi, t_lo], axis=0), spread, preferred_element_type=F32)
    total = jnp.where(
        jnp.right_shift(lane16, 4) == jnp.bitwise_and(row16, 7), total[:16] + total[16:], 0.0
    )
    mine = jnp.concatenate(
        [jnp.sum(total[:8], axis=0, keepdims=True), jnp.sum(total[8:], axis=0, keepdims=True)], axis=0
    )
    part[...] = mine
    zb[slot] = mine
    n_zb = fresh()
    for device in line:
        remote(part, zb.at[slot], device, n_zb)

    for c in go_right + go_left + go_mate + side:
        c.wait_recv()
    hop_right = [remote(conds.at[2, 0], conds.at[1, 0], right), remote(blocks.at[2, 0], blocks.at[1, 0], right)]
    hop_left = [remote(conds.at[4, 0], conds.at[5, 0], left), remote(blocks.at[4, 0], blocks.at[5, 0], left)]
    hop_mate = [
        remote(conds.at[2, 0], conds.at[2, 1], mate), remote(blocks.at[2, 0], blocks.at[2, 1], mate),
        remote(conds.at[4, 0], conds.at[4, 1], mate), remote(blocks.at[4, 0], blocks.at[4, 1], mate),
    ]
    loads[4].wait()
    loads[5].wait()

    lane32 = lax.broadcasted_iota(jnp.int32, (32, LAT), 1)
    low32, high32 = lane32 == 0, lane32 == LAT - 1
    is_low = ((1 - h).astype(F32), h.astype(F32))
    is_high = (h.astype(F32), (1 - h).astype(F32))

    def north(d, c):
        return conds[d + 3, c, 0] * jnp.where(s + d == 0, 0.0, 1.0)

    def south(d, c):
        return conds[d + 3, c, 1] * jnp.where(s + d == ring - 1, 0.0, 1.0)

    def widen(source, target, level):
        there = lambda d, c: abs(d) <= level - c
        for c in (0, 1):
            for d in range(c - level - 1, level + 2 - c):
                for i in range(0, LAT, 32):
                    rows = pl.ds(i, 32)
                    terms = []
                    if there(d + 1, c):
                        terms.append(source(d + 1, c)[rows] * north(d + 1, c))
                    if there(d - 1, c):
                        terms.append(source(d - 1, c)[rows] * south(d - 1, c))
                    w, e = None, None
                    if there(d, c):
                        me = source(d, c)[rows]
                        w, e = me * conds[d + 3, c, 2], me * conds[d + 3, c, 3]
                    if there(d, 1 - c):
                        ot = source(d, 1 - c)[rows]
                        zero = jnp.zeros_like(ot)
                        w = jnp.where(low32, ot * (conds[d + 3, 1 - c, 2] * is_low[c]), zero if w is None else w)
                        e = jnp.where(high32, ot * (conds[d + 3, 1 - c, 3] * is_high[c]), zero if e is None else e)
                    elif w is not None:
                        w, e = jnp.where(low32, 0.0, w), jnp.where(high32, 0.0, e)
                    if w is not None:
                        terms += [pltpu.roll(w, LAT - 1, 1), pltpu.roll(e, 1, 1)]
                    k_hi, k_lo = split2(sum(terms[1:], terms[0]))
                    kk[rows, :] = jnp.concatenate([k_hi, k_hi, k_lo], axis=1)
                b_hi, b_lo = split2(blocks[d + 3, c])
                q = jnp.dot(kk[...], jnp.concatenate([b_hi, b_lo, b_hi], axis=0), preferred_element_type=F32)
                if target is not None:
                    target[d + 3, c] = q
                if there(d, c):
                    green[d + 3, c] += q
                else:
                    green[d + 3, c] = q

    green[3, 0] = blocks[3, 0]
    widen(lambda d, c: blocks.at[d + 3, c], qb, 0)
    radial_pass(xr, acc)
    for c in copies:
        c.wait_recv()
    lon_pass(xt, acct)

    def section_one(l, carry):
        for v in range(8):
            yr[v, l + 2] = xr[v, l + 2] - (0.5 * TIME_STEP) * (acc[v, l] + acct[v, :, l, :])
        return carry

    lax.fori_loop(0, R, section_one, 0)
    for v in range(8):
        turn(yt, yr, v)
        e = yr[v, 2 + 15 * h]
        yr[v, edge] = e
        yr[v, edge + 1] = e

    landed(zb.at[pl.ds(0, 15)], n_zb)
    columns = jnp.concatenate([zb[2 * k] + zb[2 * k + 1] for k in range(NZ)], axis=0)
    row128 = lax.broadcasted_iota(jnp.int32, (LAT, LAT), 0)
    lane128 = lax.broadcasted_iota(jnp.int32, (LAT, LAT), 1)
    placed = jnp.where(
        jnp.right_shift(row128, 4) == xy % 8, jnp.concatenate([columns] * 8, axis=0), 0.0
    )
    pick = jnp.where(lane128 == row128 + (z - REACH), 1.0, 0.0).astype(BF16)
    p_hi, p_lo = split2(placed)
    a1s[...] = (nt(pick, p_hi) + nt(pick, p_lo)).reshape(NXY, 8, LAT)
    n_a1 = fresh()
    for to, device in plane:
        remote(a1s.at[to], a1.at[xy], device, n_a1)
    a1[xy] = a1s[xy]

    for c in hop_right + hop_left + hop_mate:
        c.wait_recv()
    end_right = [remote(blocks.at[1, 0], blocks.at[0, 0], right)]
    end_left = [remote(blocks.at[5, 0], blocks.at[6, 0], left)]
    end_mate = [remote(blocks.at[1, 0], blocks.at[1, 1], mate), remote(blocks.at[5, 0], blocks.at[5, 1], mate)]
    again = [
        remote(yr.at[:, pl.ds(2 + low, 2)], yr.at[:, pl.ds(edge, 2)], mate),
        remote(yt.at[:, pl.ds(8, 2)], yt.at[:, pl.ds(0, 2)], right),
        remote(yt.at[:, pl.ds(2, 2)], yt.at[:, pl.ds(10, 2)], left),
    ]
    widen(lambda d, c: qb.at[d + 3, c], qa, 1)
    for c in end_right + end_left + end_mate:
        c.wait_recv()
    widen(lambda d, c: qa.at[d + 3, c], None, 2)

    landed(a1.at[pl.ds(0, 15)], n_a1)
    out = jnp.zeros((LAT, LAT), F32)
    for c in (0, 1):
        first_source = 8 * h if c == 0 else 8 * (1 - h)
        rows = a1[first_source]
        for k in range(1, 8):
            rows = rows + a1[first_source + k]
        for d in range(c - REACH, REACH + 1 - c):
            out = out + green[d + 3, c] * jnp.broadcast_to(rows[d + 3 : d + 4], (LAT, LAT))
    o_hi, o_lo = split2(out)
    all_ones = jnp.ones((16, LAT), BF16)
    potential = (nt(all_ones, o_hi) + nt(all_ones, o_lo))[:1]
    out_pot[...] = potential
    prow[...] = potential
    zp[slot] = potential
    n_zp = fresh()
    for device in line:
        remote(prow, zp.at[slot], device, n_zp)

    lat_pass(yr, 2, acc)

    landed(zp.at[pl.ds(0, 15)], n_zp)
    lines = jnp.concatenate(
        [jnp.concatenate([zp[2 * k], zp[2 * k + 1]], axis=1) for k in range(NZ)], axis=0
    )
    row256 = lax.broadcasted_iota(jnp.int32, (LAT, 2 * LAT), 0)
    placed = jnp.where(jnp.right_shift(row256, 3) == xy, jnp.concatenate([lines] * NXY, axis=0), 0.0)
    m = lax.broadcasted_iota(jnp.int32, (2 * NXY, 2 * LAT), 0)
    n = lax.broadcasted_iota(jnp.int32, (2 * NXY, 2 * LAT), 1)
    pick2 = jnp.where(
        n == 2 * (jnp.right_shift(m, 1) * NZ + z) + jnp.bitwise_and(m, 1), 1.0, 0.0
    ).astype(BF16)
    l_hi, l_lo = split2(placed)
    picked = nt(pick2, l_hi) + nt(pick2, l_lo)
    for k in range(NXY):
        a2s[k] = picked[2 * k : 2 * k + 2]
    n_a2 = fresh()
    for to, device in plane:
        remote(a2s.at[to], a2.at[xy], device, n_a2)
    a2[xy] = a2s[xy]

    for c in again:
        c.wait_recv()
    radial_pass(yr, acc)
    lon_pass(yt, acct)

    def last_step(l, carry):
        for v in range(8):
            out_state[v, l] = 0.5 * (
                xr[v, l + 2] + yr[v, l + 2] - (0.5 * TIME_STEP) * (acc[v, l] + acct[v, :, l, :])
            )
        return carry

    lax.fori_loop(0, R, last_step, 0)

    landed(a2.at[pl.ds(0, 15)], n_a2)
    table = a2[0]
    for k in range(1, NXY):
        table = table + a2[k]
    out_table[...] = table

    for c in (
        near + copies + side + again + go_right + go_left + go_mate + hop_right + hop_left + hop_mate
        + end_right + end_left + end_mate
    ):
        c.wait_send()
    sent(zb.at[pl.ds(0, 15)], n_zb)
    sent(a1.at[pl.ds(0, 15)], n_a1)
    sent(zp.at[pl.ds(0, 15)], n_zp)
    sent(a2.at[pl.ds(0, 15)], n_a2)
    assert count[0] <= N_SEMS, count[0]


def finish(state, pot, table, foot, out_state, out_pot, out_foot, buf, sem):
    copies = [
        pltpu.make_async_copy(state, out_state, sem.at[0]),
        pltpu.make_async_copy(pot, out_pot, sem.at[1]),
    ]
    for c in copies:
        c.start()
    tab0 = jnp.broadcast_to(table[0:1, :], (LON, LAT))
    tab1 = jnp.broadcast_to(table[1:2, :], (LON, LAT))
    for l in range(R):
        node = foot[l]
        row = jnp.right_shift(node, 8)
        buf[l] = jnp.where(
            jnp.bitwise_and(node, 1) == 0,
            jnp.take_along_axis(tab0, row, axis=1, mode="promise_in_bounds"),
            jnp.take_along_axis(tab1, row, axis=1, mode="promise_in_bounds"),
        )
    copies.append(pltpu.make_async_copy(buf, out_foot, sem.at[2]))
    copies[2].start()
    for c in copies:
        c.wait()


N_SEMS = 48


def body(state, footpoints, conductance, inverse_blocks):
    vmem = pl.BlockSpec(memory_space=pltpu.VMEM)
    hbm = pl.BlockSpec(memory_space=pltpu.HBM)
    whole = (
        jax.ShapeDtypeStruct((8, R, LON, LAT), F32),
        jax.ShapeDtypeStruct((1, LAT), F32),
    )
    cells, potential, table = pl.pallas_call(
        kernel,
        out_shape=whole + (jax.ShapeDtypeStruct((2, LAT), F32),),
        in_specs=[hbm] * 4,
        out_specs=(vmem, vmem, vmem),
        scratch_shapes=[
            pltpu.VMEM((R, LON, LAT), jnp.int32),
            pltpu.VMEM((8, R + 4, LON, LAT), F32),
            pltpu.VMEM((8, LON + 4, R, LAT), F32),
            pltpu.VMEM((8, R + 4, LON, LAT), F32),
            pltpu.VMEM((8, LON + 4, R, LAT), F32),
            pltpu.VMEM((8, R, LON, LAT), F32),
            pltpu.VMEM((8, LON, R, LAT), F32),
            pltpu.VMEM((2, LON, R, LAT), F32),
            pltpu.VMEM((2, 2, R, LAT), F32),
            pltpu.VMEM((2, LAT), F32),
            pltpu.VMEM((16, 2, LAT), F32),
            pltpu.VMEM((NXY, 8, LAT), F32),
            pltpu.VMEM((NXY, 8, LAT), F32),
            pltpu.VMEM((1, LAT), F32),
            pltpu.VMEM((16, 1, LAT), F32),
            pltpu.VMEM((NXY, 2, LAT), F32),
            pltpu.VMEM((NXY, 2, LAT), F32),
            pltpu.VMEM((7, 2, LAT, LAT), F32),
            pltpu.VMEM((7, 2, 4, 1, LAT), F32),
            pltpu.VMEM((7, 2, LAT, LAT), F32),
            pltpu.VMEM((7, 2, LAT, LAT), F32),
            pltpu.VMEM((7, 2, LAT, LAT), F32),
            pltpu.VMEM((LAT, 3 * LAT), BF16),
            pltpu.SemaphoreType.DMA((N_SEMS,)),
            pltpu.SemaphoreType.DMA((N_SEMS,)),
            pltpu.SemaphoreType.DMA((6,)),
        ],
        compiler_params=pltpu.CompilerParams(
            collective_id=0, has_side_effects=True, vmem_limit_bytes=40 << 20
        ),
    )(*(pltpu.with_memory_space_constraint(a, pltpu.HBM) for a in (state, footpoints, conductance, inverse_blocks)))
    return pl.pallas_call(
        finish,
        out_shape=whole + (jax.ShapeDtypeStruct((R, LON, LAT), F32),),
        in_specs=[vmem] * 4,
        out_specs=(hbm, hbm, hbm),
        scratch_shapes=[pltpu.VMEM((R, LON, LAT), F32), pltpu.SemaphoreType.DMA((3,))],
        compiler_params=pltpu.CompilerParams(vmem_limit_bytes=8 << 20),
    )(cells, potential, table, footpoints)


def solution(mesh):
    return jax.shard_map(
        body,
        mesh=mesh,
        in_specs=(
            P(None, "radial", "shell", None),
            P("radial", "shell", None),
            P(None, "shell", "radial"),
            P("shell", "radial", None, None),
        ),
        out_specs=(
            P(None, "radial", "shell", None),
            P("shell", "radial"),
            P("radial", "shell", None),
        ),
        check_vma=False,
    )
```

```python
import jax
import jax.numpy as jnp
from jax import lax
from jax.experimental import pallas as pl
from jax.experimental.pallas import tpu as pltpu
from jax.sharding import PartitionSpec as P

F32 = jnp.float32
BF16 = jnp.bfloat16
GAMMA = 5.0 / 3.0
TIME_STEP = 0.02
CELL_AREA = 0.125
REACH = 3

NZ = 8
NXY = 16
R = 16
LON = 8
LAT = 128
FAR_FIRST_Z = (4, 3, 5, 2, 6, 1, 7)
FAR_FIRST_XY = (10, 6, 14, 2, 9, 11, 5, 7, 13, 15, 1, 3, 8, 4, 12)

NT = (((1,), (1,)), ((), ()))
MESH = pl.DeviceIdType.MESH


def minmod(a, b):
    return jnp.maximum(jnp.minimum(a, jnp.maximum(b, 0.0)), jnp.minimum(b, 0.0))


def flux(u, d):
    density, energy = u[0], u[7]
    inv = 1.0 / density
    vel = [u[1] * inv, u[2] * inv, u[3] * inv]
    mag = u[4:7]
    field_sq = mag[0] * mag[0] + mag[1] * mag[1] + mag[2] * mag[2]
    kinetic = vel[0] * vel[0] + vel[1] * vel[1] + vel[2] * vel[2]
    half_sq = 0.5 * field_sq
    pressure = (GAMMA - 1.0) * (energy - 0.5 * density * kinetic - half_sq)
    total = pressure + half_sq
    vn, bn = vel[d], mag[d]
    align = vel[0] * mag[0] + vel[1] * mag[1] + vel[2] * mag[2]
    out = [u[1 + d]]
    for k in range(3):
        m = u[1 + k] * vn - mag[k] * bn
        out.append(m + total if k == d else m)
    for k in range(3):
        out.append(None if k == d else vn * mag[k] - bn * vel[k])
    out.append((energy + total) * vn - bn * align)
    signal = jnp.abs(vn) + jnp.sqrt((GAMMA * jnp.abs(pressure) + field_sq) * inv)
    return out, signal


def face(left, right, d):
    fl, sl = flux(left, d)
    fr, sr = flux(right, d)
    top = jnp.maximum(sl, sr)
    out = []
    for k in range(8):
        jump = top * (right[k] - left[k])
        out.append(-jump if fl[k] is None else (fl[k] + fr[k]) - jump)
    return out


def split2(x):
    hi = x.astype(BF16)
    lo = (x - hi.astype(F32)).astype(BF16)
    return hi, lo


def nt(a, b):
    return lax.dot_general(a, b, NT, preferred_element_type=F32)


def lat_pass(src, base, acc):
    lane = lax.broadcasted_iota(jnp.int32, (4, LON, LAT), 2)
    last, first = lane == LAT - 1, lane == 0

    def step(i, carry):
        l = i * 4
        left, right = [], []
        for v in range(8):
            u = src[v, pl.ds(base + l, 4)]
            d = jnp.where(last, 0.0, pltpu.roll(u, LAT - 1, 2) - u)
            h = 0.5 * minmod(d, pltpu.roll(d, 1, 2))
            left.append(u + h)
            r = u - h
            right.append(jnp.where(last, r, pltpu.roll(r, LAT - 1, 2)))
        fl, sl = flux(left, 2)
        fr, sr = flux(right, 2)
        top = jnp.maximum(sl, sr)
        for v in range(8):
            jump = top * (right[v] - left[v])
            if fl[v] is None:
                f = -jump
                acc[v, pl.ds(l, 4)] = f - jnp.where(first, 0.0, pltpu.roll(f, 1, 2))
            else:
                f = (fl[v] + fr[v]) - jump
                acc[v, pl.ds(l, 4)] = f - jnp.where(first, 2.0 * fl[v], pltpu.roll(f, 1, 2))
        return carry

    lax.fori_loop(0, R // 4, step, 0)


def radial_pass(ext, acc):
    half = R // 2

    def cells(i):
        return [jnp.stack([ext[v, i], ext[v, i + half]]) for v in range(8)]

    def advance(f, prev, here):
        nxt = cells(f + 2)
        left, right, jumps = [], [], []
        for v in range(8):
            d = nxt[v] - here[v]
            h = 0.5 * minmod(d, prev[v])
            jumps.append(d)
            left.append(here[v] + h)
            right.append(here[v] - h)
        return nxt, jumps, left, right

    c0, c1 = cells(0), cells(1)
    prev = [c1[v] - c0[v] for v in range(8)]
    here, prev, left, _ = advance(0, prev, c1)
    here, prev, left2, right = advance(1, prev, here)
    f0 = face(left, right, 0)

    def step(i, carry):
        here, prev, left, f0 = carry
        here, prev, left2, right = advance(i + 2, prev, here)
        f1 = face(left, right, 0)
        for v in range(8):
            df = f1[v] - f0[v]
            acc[v, i] += df[0]
            acc[v, i + half] += df[1]
        return here, prev, left2, f1

    lax.fori_loop(0, half, step, (here, prev, left2, f0))


def lon_pass(ext, acc):
    def advance(i, prev, here):
        left, right, jumps, nxt = [], [], [], []
        for v in range(8):
            n = ext[v, i]
            d = n - here[v]
            h = 0.5 * minmod(d, prev[v])
            nxt.append(n)
            jumps.append(d)
            left.append(here[v] + h)
            right.append(here[v] - h)
        return nxt, jumps, left, right

    c0 = [ext[v, 0] for v in range(8)]
    c1 = [ext[v, 1] for v in range(8)]
    prev = [c1[v] - c0[v] for v in range(8)]
    here, prev, left, _ = advance(2, prev, c1)
    here, prev, left2, right = advance(3, prev, here)
    f0 = face(left, right, 1)

    def step(i, carry):
        here, prev, left, f0 = carry
        here, prev, left2, right = advance(i + 4, prev, here)
        f1 = face(left, right, 1)
        for v in range(8):
            acc[v, i] = f1[v] - f0[v]
        return here, prev, left2, f1

    lax.fori_loop(0, LON, step, (here, prev, left2, f0))


def kernel(
    state, foot_hbm, cond, inv,
    out_state, out_pot, out_table,
    foot, xr, xt, yr, yt, acc, acct, dt1, edge_in,
    part, zb, a1s, a1, prow, zp, a2s, a2,
    blocks, conds, qa, qb, green, kk,
    send_sem, recv_sem, local_sem,
):
    s = lax.axis_index("shell")
    h = lax.axis_index("radial")
    ring = NZ * NXY
    z, xy = s % NZ, s // NZ
    base = s - z
    right = ((s + 1) % ring, h)
    left = ((s + ring - 1) % ring, h)
    mate = (s, 1 - h)
    right2 = ((s + 2) % ring, h)
    left2 = ((s + ring - 2) % ring, h)
    line = [(base + (z + k) % NZ, c) for k in FAR_FIRST_Z for c in (0, 1)] + [mate]
    plane = [((xy + k) % NXY, ((xy + k) % NXY * NZ + z, h)) for k in FAR_FIRST_XY]
    slot = z * 2 + h
    count = [0]

    def fresh():
        count[0] += 1
        return count[0] - 1

    def remote(src, dst, device, n=None):
        n = fresh() if n is None else n
        copy = pltpu.make_async_remote_copy(
            src_ref=src, dst_ref=dst, send_sem=send_sem.at[n], recv_sem=recv_sem.at[n],
            device_id=device, device_id_type=MESH,
        )
        copy.start()
        return copy

    def landed(ref, n):
        pltpu.make_async_copy(ref, ref, recv_sem.at[n]).wait()

    def sent(ref, n):
        pltpu.make_async_copy(ref, ref, send_sem.at[n]).wait()

    barrier = pltpu.get_barrier_semaphore()
    partners = [p for _, p in plane[:5]] + line[:6] + [right2, left2, right, left] + [p for _, p in plane[5:]] + line[6:]
    for device in partners:
        pl.semaphore_signal(barrier, inc=1, device_id=device, device_id_type=MESH)

    inner = pl.ds(2, R)
    loads = [
        pltpu.make_async_copy(state.at[pl.ds(4, 3)], xr.at[pl.ds(4, 3), inner], local_sem.at[0]),
        pltpu.make_async_copy(state.at[pl.ds(0, 4)], xr.at[pl.ds(0, 4), inner], local_sem.at[1]),
        pltpu.make_async_copy(state.at[pl.ds(7, 1)], xr.at[pl.ds(7, 1), inner], local_sem.at[2]),
        pltpu.make_async_copy(foot_hbm, foot, local_sem.at[3]),
        pltpu.make_async_copy(inv.at[0, 0], blocks.at[3, 0], local_sem.at[4]),
        pltpu.make_async_copy(cond, conds.at[3, 0], local_sem.at[5]),
    ]
    for c in loads:
        c.start()

    def turn(dst, src, v):
        for j in range(LON):
            dst[v, j + 2] = src[v, 2 : R + 2, j, :]

    pl.semaphore_wait(barrier, len(partners))

    edge, low = 18 * h, 14 * (1 - h)
    copies, near = [], []
    for k, v in enumerate((6, 4)):
        near.append(remote(state.at[v, :, LON - 1, :], edge_in.at[k, 0], right))
        near.append(remote(state.at[v, :, 0, :], edge_in.at[k, 1], left))
    near.append(remote(state.at[pl.ds(4, 3), pl.ds(low, 2)], xr.at[pl.ds(4, 3), pl.ds(edge, 2)], mate))

    own_block, own_cond = inv.at[0, 0], cond
    go_right = [remote(own_cond, conds.at[2, 0], right), remote(own_block, blocks.at[2, 0], right)]
    go_left = [remote(own_cond, conds.at[4, 0], left), remote(own_block, blocks.at[4, 0], left)]
    go_mate = [remote(own_cond, conds.at[3, 1], mate), remote(own_block, blocks.at[3, 1], mate)]
    for j in (0, 1):
        copies.append(remote(state.at[:, :, 6 + j, :], xt.at[:, j], right))
        copies.append(remote(state.at[:, :, j, :], xt.at[:, 10 + j], left))
    hop_right = [remote(own_cond, conds.at[1, 0], right2), remote(own_block, blocks.at[1, 0], right2)]
    hop_left = [remote(own_cond, conds.at[5, 0], left2), remote(own_block, blocks.at[5, 0], left2)]
    side = [
        remote(state.at[pl.ds(0, 4), pl.ds(low, 2)], xr.at[pl.ds(0, 4), pl.ds(edge, 2)], mate),
        remote(state.at[pl.ds(7, 1), pl.ds(low, 2)], xr.at[pl.ds(7, 1), pl.ds(edge, 2)], mate),
    ]

    loads[0].wait()
    for v in (4, 6):
        turn(xt, xr, v)
    loads[1].wait()
    loads[2].wait()
    for v in (5, 0, 1, 2, 3, 7):
        turn(xt, xr, v)
    for v in range(8):
        e = xr[v, 2 + 15 * h]
        xr[v, edge] = e
        xr[v, edge + 1] = e
    lat_pass(xr, 2, acc)

    loads[3].wait()
    for c in near:
        c.wait_recv()
    for k, v in enumerate((6, 4)):
        dt1[k, 0] = xt[v, 3] - edge_in[k, 0]
        for j in range(1, LON - 1):
            dt1[k, j] = xt[v, j + 3] - xt[v, j + 1]
        dt1[k, LON - 1] = edge_in[k, 1] - xt[v, LON]
    lane = lax.broadcasted_iota(jnp.int32, (LON, LAT), 1)
    first, last = lane == 0, lane == LAT - 1
    row16 = lax.broadcasted_iota(jnp.int32, (16, LAT), 0)
    lane16 = lax.broadcasted_iota(jnp.int32, (16, LAT), 1)

    def along_lat(b):
        up = jnp.where(last, b, pltpu.roll(b, LAT - 1, 1))
        down = jnp.where(first, b, pltpu.roll(b, 1, 1))
        return up - down

    def current_step(i, total):
        a, ones = [], []
        for t in range(4):
            l = i * 4 + t
            b = [xr[v, l + 2] for v in (4, 5, 6)]
            up = [xr[v, l + 3] for v in (5, 6)]
            dn = [xr[v, l + 1] for v in (5, 6)]
            c0 = dt1[0, :, l, :] - along_lat(b[1])
            c1 = along_lat(b[0]) - (up[1] - dn[1])
            c2 = (up[0] - dn[0]) - dt1[1, :, l, :]
            sq = b[0] * b[0] + b[1] * b[1] + b[2] * b[2]
            val = (0.5 * CELL_AREA) * (c0 * b[0] + c1 * b[1] + c2 * b[2]) / jnp.sqrt(1.0 + sq)
            hi = val.astype(BF16).astype(F32)
            lo = val - hi
            node = foot[l]
            row = jnp.right_shift(node, 8)
            group = jnp.bitwise_and(node, 1) * 8 + jnp.right_shift(row, 4)
            within = jnp.bitwise_and(row, 15)
            for j in range(LON):
                hit = jnp.broadcast_to(group[j : j + 1], (16, LAT)) == row16
                top = jnp.where(hit, jnp.broadcast_to(hi[j : j + 1], (16, LAT)), 0.0)
                low_part = jnp.where(hit, jnp.broadcast_to(lo[j : j + 1], (16, LAT)), 0.0)
                a.append(jnp.concatenate([top.astype(BF16), low_part.astype(BF16)], axis=0))
                one = jnp.where(jnp.broadcast_to(within[j : j + 1], (16, LAT)) == row16, 1.0, 0.0)
                ones.append(one.astype(BF16))
        return total + nt(jnp.concatenate(a, axis=1), jnp.concatenate(ones, axis=1))

    total = lax.fori_loop(0, R // 4, current_step, jnp.zeros((32, 16), F32))
    spread = jnp.where(jnp.bitwise_and(lane16, 15) == row16, 1.0, 0.0).astype(BF16)
    t_hi, t_lo = split2(total[:16] + total[16:])
    total = jnp.dot(jnp.concatenate([t_hi, t_lo], axis=0), spread, preferred_element_type=F32)
    total = jnp.where(
        jnp.right_shift(lane16, 4) == jnp.bitwise_and(row16, 7), total[:16] + total[16:], 0.0
    )
    mine = jnp.concatenate(
        [jnp.sum(total[:8], axis=0, keepdims=True), jnp.sum(total[8:], axis=0, keepdims=True)], axis=0
    )
    part[...] = mine
    zb[slot] = mine
    n_zb = fresh()
    for device in line:
        remote(part, zb.at[slot], device, n_zb)

    for c in go_right + go_left + go_mate + side:
        c.wait_recv()
    hop_mate = [
        remote(conds.at[2, 0], conds.at[2, 1], mate), remote(blocks.at[2, 0], blocks.at[2, 1], mate),
        remote(conds.at[4, 0], conds.at[4, 1], mate), remote(blocks.at[4, 0], blocks.at[4, 1], mate),
    ]
    loads[4].wait()
    loads[5].wait()

    lane32 = lax.broadcasted_iota(jnp.int32, (32, LAT), 1)
    low32, high32 = lane32 == 0, lane32 == LAT - 1
    is_low = ((1 - h).astype(F32), h.astype(F32))
    is_high = (h.astype(F32), (1 - h).astype(F32))

    def north(d, c):
        return conds[d + 3, c, 0] * jnp.where(s + d == 0, 0.0, 1.0)

    def south(d, c):
        return conds[d + 3, c, 1] * jnp.where(s + d == ring - 1, 0.0, 1.0)

    def widen(source, target, level):
        there = lambda d, c: abs(d) <= level - c
        for c in (0, 1):
            for d in range(c - level - 1, level + 2 - c):
                for i in range(0, LAT, 32):
                    rows = pl.ds(i, 32)
                    terms = []
                    if there(d + 1, c):
                        terms.append(source(d + 1, c)[rows] * north(d + 1, c))
                    if there(d - 1, c):
                        terms.append(source(d - 1, c)[rows] * south(d - 1, c))
                    w, e = None, None
                    if there(d, c):
                        me = source(d, c)[rows]
                        w, e = me * conds[d + 3, c, 2], me * conds[d + 3, c, 3]
                    if there(d, 1 - c):
                        ot = source(d, 1 - c)[rows]
                        zero = jnp.zeros_like(ot)
                        w = jnp.where(low32, ot * (conds[d + 3, 1 - c, 2] * is_low[c]), zero if w is None else w)
                        e = jnp.where(high32, ot * (conds[d + 3, 1 - c, 3] * is_high[c]), zero if e is None else e)
                    elif w is not None:
                        w, e = jnp.where(low32, 0.0, w), jnp.where(high32, 0.0, e)
                    if w is not None:
                        terms += [pltpu.roll(w, LAT - 1, 1), pltpu.roll(e, 1, 1)]
                    k_hi, k_lo = split2(sum(terms[1:], terms[0]))
                    kk[rows, :] = jnp.concatenate([k_hi, k_hi, k_lo], axis=1)
                b_hi, b_lo = split2(blocks[d + 3, c])
                q = jnp.dot(kk[...], jnp.concatenate([b_hi, b_lo, b_hi], axis=0), preferred_element_type=F32)
                if target is not None:
                    target[d + 3, c] = q
                if there(d, c):
                    green[d + 3, c] += q
                else:
                    green[d + 3, c] = q

    green[3, 0] = blocks[3, 0]
    widen(lambda d, c: blocks.at[d + 3, c], qb, 0)
    radial_pass(xr, acc)
    for c in hop_right + hop_left:
        c.wait_recv()
    end_right = [remote(blocks.at[1, 0], blocks.at[0, 0], right)]
    end_left = [remote(blocks.at[5, 0], blocks.at[6, 0], left)]
    end_mate = [remote(blocks.at[1, 0], blocks.at[1, 1], mate), remote(blocks.at[5, 0], blocks.at[5, 1], mate)]
    row128 = lax.broadcasted_iota(jnp.int32, (LAT, LAT), 0)
    lane128 = lax.broadcasted_iota(jnp.int32, (LAT, LAT), 1)
    pick = jnp.where(lane128 == row128 + (z - REACH), 1.0, 0.0).astype(BF16)
    landed(zb.at[pl.ds(0, 15)], n_zb)
    columns = jnp.concatenate([zb[2 * k] + zb[2 * k + 1] for k in range(NZ)], axis=0)
    p_hi, p_lo = split2(columns)
    seven = nt(pick, p_hi) + nt(pick, p_lo)
    seven = jnp.concatenate([seven, jnp.zeros((LAT, LAT - 16), F32)], axis=1)
    a1s[...] = pltpu.roll(seven, (xy % 8) * 16, 1).reshape(NXY, 8, LAT)
    n_a1 = fresh()
    for to, device in plane:
        remote(a1s.at[to], a1.at[xy], device, n_a1)
    a1[xy] = a1s[xy]


    for c in hop_mate:
        c.wait_recv()
    widen(lambda d, c: qb.at[d + 3, c], qa, 1)
    for c in copies:
        c.wait_recv()
    lon_pass(xt, acct)

    def section_one(l, carry):
        for v in range(8):
            yr[v, l + 2] = xr[v, l + 2] - (0.5 * TIME_STEP) * (acc[v, l] + acct[v, :, l, :])
        return carry

    lax.fori_loop(0, R, section_one, 0)
    for v in range(8):
        turn(yt, yr, v)
        e = yr[v, 2 + 15 * h]
        yr[v, edge] = e
        yr[v, edge + 1] = e
    again = [
        remote(yr.at[:, pl.ds(2 + low, 2)], yr.at[:, pl.ds(edge, 2)], mate),
        remote(yt.at[:, pl.ds(8, 2)], yt.at[:, pl.ds(0, 2)], right),
        remote(yt.at[:, pl.ds(2, 2)], yt.at[:, pl.ds(10, 2)], left),
    ]
    for c in end_right + end_left + end_mate:
        c.wait_recv()
    widen(lambda d, c: qa.at[d + 3, c], None, 2)

    landed(a1.at[pl.ds(0, 15)], n_a1)
    out = jnp.zeros((LAT, LAT), F32)
    for c in (0, 1):
        first_source = 8 * h if c == 0 else 8 * (1 - h)
        rows = a1[first_source]
        for k in range(1, 8):
            rows = rows + a1[first_source + k]
        for d in range(c - REACH, REACH + 1 - c):
            out = out + green[d + 3, c] * jnp.broadcast_to(rows[d + 3 : d + 4], (LAT, LAT))
    o_hi, o_lo = split2(out)
    all_ones = jnp.ones((16, LAT), BF16)
    potential = (nt(all_ones, o_hi) + nt(all_ones, o_lo))[:1]
    out_pot[...] = potential
    prow[...] = potential
    zp[slot] = potential
    n_zp = fresh()
    for device in line:
        remote(prow, zp.at[slot], device, n_zp)

    lat_pass(yr, 2, acc)

    m = lax.broadcasted_iota(jnp.int32, (2 * NXY, 2 * LAT), 0)
    n = lax.broadcasted_iota(jnp.int32, (2 * NXY, 2 * LAT), 1)
    pick2 = jnp.where(
        n == 2 * (jnp.right_shift(m, 1) * NZ + z) + jnp.bitwise_and(m, 1), 1.0, 0.0
    ).astype(BF16)
    landed(zp.at[pl.ds(0, 15)], n_zp)
    lines = jnp.concatenate(
        [jnp.concatenate([zp[2 * k], zp[2 * k + 1]], axis=1) for k in range(NZ)], axis=0
    )
    l_hi, l_lo = split2(lines)
    picked = nt(pick2, l_hi) + nt(pick2, l_lo)
    picked = jnp.concatenate([picked, jnp.zeros((2 * NXY, LAT - NZ), F32)], axis=1)
    picked = pltpu.roll(picked, xy * NZ, 1)
    for k in range(NXY):
        a2s[k] = picked[2 * k : 2 * k + 2]
    n_a2 = fresh()
    for to, device in plane:
        remote(a2s.at[to], a2.at[xy], device, n_a2)
    a2[xy] = a2s[xy]

    for c in again:
        c.wait_recv()
    radial_pass(yr, acc)
    lon_pass(yt, acct)

    def last_step(l, carry):
        for v in range(8):
            out_state[v, l] = 0.5 * (
                xr[v, l + 2] + yr[v, l + 2] - (0.5 * TIME_STEP) * (acc[v, l] + acct[v, :, l, :])
            )
        return carry

    lax.fori_loop(0, R, last_step, 0)

    landed(a2.at[pl.ds(0, 15)], n_a2)
    table = a2[0]
    for k in range(1, NXY):
        table = table + a2[k]
    out_table[...] = table

    for c in (
        near + copies + side + again + go_right + go_left + go_mate + hop_right + hop_left + hop_mate
        + end_right + end_left + end_mate
    ):
        c.wait_send()
    sent(zb.at[pl.ds(0, 15)], n_zb)
    sent(a1.at[pl.ds(0, 15)], n_a1)
    sent(zp.at[pl.ds(0, 15)], n_zp)
    sent(a2.at[pl.ds(0, 15)], n_a2)
    assert count[0] <= N_SEMS, count[0]


def finish(state, pot, table, foot, out_state, out_pot, out_foot, buf, sem):
    copies = [
        pltpu.make_async_copy(state, out_state, sem.at[0]),
        pltpu.make_async_copy(pot, out_pot, sem.at[1]),
    ]
    for c in copies:
        c.start()
    tab0 = jnp.broadcast_to(table[0:1, :], (LON, LAT))
    tab1 = jnp.broadcast_to(table[1:2, :], (LON, LAT))
    for l in range(R):
        node = foot[l]
        row = jnp.right_shift(node, 8)
        buf[l] = jnp.where(
            jnp.bitwise_and(node, 1) == 0,
            jnp.take_along_axis(tab0, row, axis=1, mode="promise_in_bounds"),
            jnp.take_along_axis(tab1, row, axis=1, mode="promise_in_bounds"),
        )
    copies.append(pltpu.make_async_copy(buf, out_foot, sem.at[2]))
    copies[2].start()
    for c in copies:
        c.wait()


N_SEMS = 52


def body(state, footpoints, conductance, inverse_blocks):
    vmem = pl.BlockSpec(memory_space=pltpu.VMEM)
    hbm = pl.BlockSpec(memory_space=pltpu.HBM)
    whole = (
        jax.ShapeDtypeStruct((8, R, LON, LAT), F32),
        jax.ShapeDtypeStruct((1, LAT), F32),
    )
    cells, potential, table = pl.pallas_call(
        kernel,
        out_shape=whole + (jax.ShapeDtypeStruct((2, LAT), F32),),
        in_specs=[hbm] * 4,
        out_specs=(vmem, vmem, vmem),
        scratch_shapes=[
            pltpu.VMEM((R, LON, LAT), jnp.int32),
            pltpu.VMEM((8, R + 4, LON, LAT), F32),
            pltpu.VMEM((8, LON + 4, R, LAT), F32),
            pltpu.VMEM((8, R + 4, LON, LAT), F32),
            pltpu.VMEM((8, LON + 4, R, LAT), F32),
            pltpu.VMEM((8, R, LON, LAT), F32),
            pltpu.VMEM((8, LON, R, LAT), F32),
            pltpu.VMEM((2, LON, R, LAT), F32),
            pltpu.VMEM((2, 2, R, LAT), F32),
            pltpu.VMEM((2, LAT), F32),
            pltpu.VMEM((16, 2, LAT), F32),
            pltpu.VMEM((NXY, 8, LAT), F32),
            pltpu.VMEM((NXY, 8, LAT), F32),
            pltpu.VMEM((1, LAT), F32),
            pltpu.VMEM((16, 1, LAT), F32),
            pltpu.VMEM((NXY, 2, LAT), F32),
            pltpu.VMEM((NXY, 2, LAT), F32),
            pltpu.VMEM((7, 2, LAT, LAT), F32),
            pltpu.VMEM((7, 2, 4, 1, LAT), F32),
            pltpu.VMEM((7, 2, LAT, LAT), F32),
            pltpu.VMEM((7, 2, LAT, LAT), F32),
            pltpu.VMEM((7, 2, LAT, LAT), F32),
            pltpu.VMEM((LAT, 3 * LAT), BF16),
            pltpu.SemaphoreType.DMA((N_SEMS,)),
            pltpu.SemaphoreType.DMA((N_SEMS,)),
            pltpu.SemaphoreType.DMA((6,)),
        ],
        compiler_params=pltpu.CompilerParams(
            collective_id=0, has_side_effects=True, vmem_limit_bytes=40 << 20
        ),
    )(*(pltpu.with_memory_space_constraint(a, pltpu.HBM) for a in (state, footpoints, conductance, inverse_blocks)))
    return pl.pallas_call(
        finish,
        out_shape=whole + (jax.ShapeDtypeStruct((R, LON, LAT), F32),),
        in_specs=[vmem] * 4,
        out_specs=(hbm, hbm, hbm),
        scratch_shapes=[pltpu.VMEM((R, LON, LAT), F32), pltpu.SemaphoreType.DMA((3,))],
        compiler_params=pltpu.CompilerParams(vmem_limit_bytes=8 << 20),
    )(cells, potential, table, footpoints)


def solution(mesh):
    return jax.shard_map(
        body,
        mesh=mesh,
        in_specs=(
            P(None, "radial", "shell", None),
            P("radial", "shell", None),
            P(None, "shell", "radial"),
            P("shell", "radial", None, None),
        ),
        out_specs=(
            P(None, "radial", "shell", None),
            P("shell", "radial"),
            P("radial", "shell", None),
        ),
        check_vma=False,
    )
```

```python
import jax
import jax.numpy as jnp
from jax import lax
from jax.experimental import pallas as pl
from jax.experimental.pallas import tpu as pltpu
from jax.sharding import PartitionSpec as P

F32 = jnp.float32
BF16 = jnp.bfloat16
GAMMA = 5.0 / 3.0
TIME_STEP = 0.02
CELL_AREA = 0.125
REACH = 3

NZ = 8
NXY = 16
R = 16
LON = 8
LAT = 128
FAR_FIRST_Z = (4, 3, 5, 2, 6, 1, 7)
FAR_FIRST_XY = (10, 6, 14, 2, 9, 11, 5, 7, 13, 15, 1, 3, 8, 4, 12)

NT = (((1,), (1,)), ((), ()))
MESH = pl.DeviceIdType.MESH


def minmod(a, b):
    return jnp.maximum(jnp.minimum(a, jnp.maximum(b, 0.0)), jnp.minimum(b, 0.0))


def flux(u, d):
    density, energy = u[0], u[7]
    inv = 1.0 / density
    vel = [u[1] * inv, u[2] * inv, u[3] * inv]
    mag = u[4:7]
    field_sq = mag[0] * mag[0] + mag[1] * mag[1] + mag[2] * mag[2]
    kinetic = vel[0] * vel[0] + vel[1] * vel[1] + vel[2] * vel[2]
    half_sq = 0.5 * field_sq
    pressure = (GAMMA - 1.0) * (energy - 0.5 * density * kinetic - half_sq)
    total = pressure + half_sq
    vn, bn = vel[d], mag[d]
    align = vel[0] * mag[0] + vel[1] * mag[1] + vel[2] * mag[2]
    out = [u[1 + d]]
    for k in range(3):
        m = u[1 + k] * vn - mag[k] * bn
        out.append(m + total if k == d else m)
    for k in range(3):
        out.append(None if k == d else vn * mag[k] - bn * vel[k])
    out.append((energy + total) * vn - bn * align)
    signal = jnp.abs(vn) + jnp.sqrt((GAMMA * jnp.abs(pressure) + field_sq) * inv)
    return out, signal


def face(left, right, d):
    fl, sl = flux(left, d)
    fr, sr = flux(right, d)
    top = jnp.maximum(sl, sr)
    out = []
    for k in range(8):
        jump = top * (right[k] - left[k])
        out.append(-jump if fl[k] is None else (fl[k] + fr[k]) - jump)
    return out


def split2(x):
    hi = x.astype(BF16)
    lo = (x - hi.astype(F32)).astype(BF16)
    return hi, lo


def nt(a, b):
    return lax.dot_general(a, b, NT, preferred_element_type=F32)


def lat_pass(src, base, acc):
    lane = lax.broadcasted_iota(jnp.int32, (4, LON, LAT), 2)
    last, first = lane == LAT - 1, lane == 0

    def step(i, carry):
        l = i * 4
        left, right = [], []
        for v in range(8):
            u = src[v, pl.ds(base + l, 4)]
            d = jnp.where(last, 0.0, pltpu.roll(u, LAT - 1, 2) - u)
            h = 0.5 * minmod(d, pltpu.roll(d, 1, 2))
            left.append(u + h)
            r = u - h
            right.append(jnp.where(last, r, pltpu.roll(r, LAT - 1, 2)))
        fl, sl = flux(left, 2)
        fr, sr = flux(right, 2)
        top = jnp.maximum(sl, sr)
        for v in range(8):
            jump = top * (right[v] - left[v])
            if fl[v] is None:
                f = -jump
                acc[v, pl.ds(l, 4)] = f - jnp.where(first, 0.0, pltpu.roll(f, 1, 2))
            else:
                f = (fl[v] + fr[v]) - jump
                acc[v, pl.ds(l, 4)] = f - jnp.where(first, 2.0 * fl[v], pltpu.roll(f, 1, 2))
        return carry

    lax.fori_loop(0, R // 4, step, 0)


def radial_pass(ext, acc):
    half = R // 2

    def cells(i):
        return [jnp.stack([ext[v, i], ext[v, i + half]]) for v in range(8)]

    def advance(f, prev, here):
        nxt = cells(f + 2)
        left, right, jumps = [], [], []
        for v in range(8):
            d = nxt[v] - here[v]
            h = 0.5 * minmod(d, prev[v])
            jumps.append(d)
            left.append(here[v] + h)
            right.append(here[v] - h)
        return nxt, jumps, left, right

    c0, c1 = cells(0), cells(1)
    prev = [c1[v] - c0[v] for v in range(8)]
    here, prev, left, _ = advance(0, prev, c1)
    here, prev, left2, right = advance(1, prev, here)
    f0 = face(left, right, 0)

    def step(i, carry):
        here, prev, left, f0 = carry
        here, prev, left2, right = advance(i + 2, prev, here)
        f1 = face(left, right, 0)
        for v in range(8):
            df = f1[v] - f0[v]
            acc[v, i] += df[0]
            acc[v, i + half] += df[1]
        return here, prev, left2, f1

    lax.fori_loop(0, half, step, (here, prev, left2, f0))


def lon_pass(ext, acc):
    def advance(i, prev, here):
        left, right, jumps, nxt = [], [], [], []
        for v in range(8):
            n = ext[v, i]
            d = n - here[v]
            h = 0.5 * minmod(d, prev[v])
            nxt.append(n)
            jumps.append(d)
            left.append(here[v] + h)
            right.append(here[v] - h)
        return nxt, jumps, left, right

    c0 = [ext[v, 0] for v in range(8)]
    c1 = [ext[v, 1] for v in range(8)]
    prev = [c1[v] - c0[v] for v in range(8)]
    here, prev, left, _ = advance(2, prev, c1)
    here, prev, left2, right = advance(3, prev, here)
    f0 = face(left, right, 1)

    def step(i, carry):
        here, prev, left, f0 = carry
        here, prev, left2, right = advance(i + 4, prev, here)
        f1 = face(left, right, 1)
        for v in range(8):
            acc[v, i] = f1[v] - f0[v]
        return here, prev, left2, f1

    lax.fori_loop(0, LON, step, (here, prev, left2, f0))


def kernel(
    state, foot_hbm, cond, inv,
    out_state, out_pot, out_table,
    foot, xr, xt, yr, yt, acc, acct, dt1, edge_in,
    part, zb, a1s, a1, prow, zp, a2s, a2,
    blocks, conds, qa, qb, green, kk,
    send_sem, recv_sem, local_sem,
):
    s = lax.axis_index("shell")
    h = lax.axis_index("radial")
    ring = NZ * NXY
    z, xy = s % NZ, s // NZ
    base = s - z
    right = ((s + 1) % ring, h)
    left = ((s + ring - 1) % ring, h)
    mate = (s, 1 - h)
    right2 = ((s + 2) % ring, h)
    left2 = ((s + ring - 2) % ring, h)
    line = [(base + (z + k) % NZ, c) for k in FAR_FIRST_Z for c in (0, 1)] + [mate]
    plane = [((xy + k) % NXY, ((xy + k) % NXY * NZ + z, h)) for k in FAR_FIRST_XY]
    slot = z * 2 + h
    count = [0]

    def fresh():
        count[0] += 1
        return count[0] - 1

    def remote(src, dst, device, n=None):
        n = fresh() if n is None else n
        copy = pltpu.make_async_remote_copy(
            src_ref=src, dst_ref=dst, send_sem=send_sem.at[n], recv_sem=recv_sem.at[n],
            device_id=device, device_id_type=MESH,
        )
        copy.start()
        return copy

    def landed(ref, n):
        pltpu.make_async_copy(ref, ref, recv_sem.at[n]).wait()

    def sent(ref, n):
        pltpu.make_async_copy(ref, ref, send_sem.at[n]).wait()

    barrier = pltpu.get_barrier_semaphore()
    partners = [p for _, p in plane[:5]] + line[:6] + [right2, left2, right, left] + [p for _, p in plane[5:]] + line[6:]
    for device in partners:
        pl.semaphore_signal(barrier, inc=1, device_id=device, device_id_type=MESH)

    inner = pl.ds(2, R)
    loads = [
        pltpu.make_async_copy(state.at[pl.ds(4, 3)], xr.at[pl.ds(4, 3), inner], local_sem.at[0]),
        pltpu.make_async_copy(state.at[pl.ds(0, 4)], xr.at[pl.ds(0, 4), inner], local_sem.at[1]),
        pltpu.make_async_copy(state.at[pl.ds(7, 1)], xr.at[pl.ds(7, 1), inner], local_sem.at[2]),
        pltpu.make_async_copy(foot_hbm, foot, local_sem.at[3]),
        pltpu.make_async_copy(inv.at[0, 0], blocks.at[3, 0], local_sem.at[4]),
        pltpu.make_async_copy(cond, conds.at[3, 0], local_sem.at[5]),
    ]
    for c in loads:
        c.start()

    def turn(dst, src, v):
        for j in range(LON):
            dst[v, j + 2] = src[v, 2 : R + 2, j, :]

    pl.semaphore_wait(barrier, len(partners))

    edge, low = 18 * h, 14 * (1 - h)
    copies, near = [], []
    for k, v in enumerate((6, 4)):
        near.append(remote(state.at[v, :, LON - 1, :], edge_in.at[k, 0], right))
        near.append(remote(state.at[v, :, 0, :], edge_in.at[k, 1], left))
    near.append(remote(state.at[pl.ds(4, 3), pl.ds(low, 2)], xr.at[pl.ds(4, 3), pl.ds(edge, 2)], mate))

    own_block, own_cond = inv.at[0, 0], cond
    go_right = [remote(own_cond, conds.at[2, 0], right), remote(own_block, blocks.at[2, 0], right)]
    go_left = [remote(own_cond, conds.at[4, 0], left), remote(own_block, blocks.at[4, 0], left)]
    go_mate = [remote(own_cond, conds.at[3, 1], mate), remote(own_block, blocks.at[3, 1], mate)]
    for j in (0, 1):
        copies.append(remote(state.at[:, :, 6 + j, :], xt.at[:, j], right))
        copies.append(remote(state.at[:, :, j, :], xt.at[:, 10 + j], left))
    hop_right = [remote(own_cond, conds.at[1, 0], right2), remote(own_block, blocks.at[1, 0], right2)]
    hop_left = [remote(own_cond, conds.at[5, 0], left2), remote(own_block, blocks.at[5, 0], left2)]
    side = [
        remote(state.at[pl.ds(0, 4), pl.ds(low, 2)], xr.at[pl.ds(0, 4), pl.ds(edge, 2)], mate),
        remote(state.at[pl.ds(7, 1), pl.ds(low, 2)], xr.at[pl.ds(7, 1), pl.ds(edge, 2)], mate),
    ]

    loads[0].wait()
    for v in (4, 6):
        turn(xt, xr, v)
    loads[1].wait()
    loads[2].wait()
    for v in (5, 0, 1, 2, 3, 7):
        turn(xt, xr, v)
    for v in range(8):
        e = xr[v, 2 + 15 * h]
        xr[v, edge] = e
        xr[v, edge + 1] = e
    lat_pass(xr, 2, acc)

    loads[3].wait()
    for c in near:
        c.wait_recv()
    for k, v in enumerate((6, 4)):
        dt1[k, 0] = xt[v, 3] - edge_in[k, 0]
        for j in range(1, LON - 1):
            dt1[k, j] = xt[v, j + 3] - xt[v, j + 1]
        dt1[k, LON - 1] = edge_in[k, 1] - xt[v, LON]
    lane = lax.broadcasted_iota(jnp.int32, (LON, LAT), 1)
    first, last = lane == 0, lane == LAT - 1
    row16 = lax.broadcasted_iota(jnp.int32, (16, LAT), 0)
    lane16 = lax.broadcasted_iota(jnp.int32, (16, LAT), 1)

    def along_lat(b):
        up = jnp.where(last, b, pltpu.roll(b, LAT - 1, 1))
        down = jnp.where(first, b, pltpu.roll(b, 1, 1))
        return up - down

    def current_step(i, total):
        a, ones = [], []
        for t in range(4):
            l = i * 4 + t
            b = [xr[v, l + 2] for v in (4, 5, 6)]
            up = [xr[v, l + 3] for v in (5, 6)]
            dn = [xr[v, l + 1] for v in (5, 6)]
            c0 = dt1[0, :, l, :] - along_lat(b[1])
            c1 = along_lat(b[0]) - (up[1] - dn[1])
            c2 = (up[0] - dn[0]) - dt1[1, :, l, :]
            sq = b[0] * b[0] + b[1] * b[1] + b[2] * b[2]
            val = (0.5 * CELL_AREA) * (c0 * b[0] + c1 * b[1] + c2 * b[2]) / jnp.sqrt(1.0 + sq)
            hi = val.astype(BF16).astype(F32)
            lo = val - hi
            node = foot[l]
            row = jnp.right_shift(node, 8)
            group = jnp.bitwise_and(node, 1) * 8 + jnp.right_shift(row, 4)
            within = jnp.bitwise_and(row, 15)
            for j in range(LON):
                hit = jnp.broadcast_to(group[j : j + 1], (16, LAT)) == row16
                top = jnp.where(hit, jnp.broadcast_to(hi[j : j + 1], (16, LAT)), 0.0)
                low_part = jnp.where(hit, jnp.broadcast_to(lo[j : j + 1], (16, LAT)), 0.0)
                a.append(jnp.concatenate([top.astype(BF16), low_part.astype(BF16)], axis=0))
                one = jnp.where(jnp.broadcast_to(within[j : j + 1], (16, LAT)) == row16, 1.0, 0.0)
                ones.append(one.astype(BF16))
        return total + nt(jnp.concatenate(a, axis=1), jnp.concatenate(ones, axis=1))

    total = lax.fori_loop(0, R // 4, current_step, jnp.zeros((32, 16), F32))
    spread = jnp.where(jnp.bitwise_and(lane16, 15) == row16, 1.0, 0.0).astype(BF16)
    t_hi, t_lo = split2(total[:16] + total[16:])
    total = jnp.dot(jnp.concatenate([t_hi, t_lo], axis=0), spread, preferred_element_type=F32)
    total = jnp.where(
        jnp.right_shift(lane16, 4) == jnp.bitwise_and(row16, 7), total[:16] + total[16:], 0.0
    )
    mine = jnp.concatenate(
        [jnp.sum(total[:8], axis=0, keepdims=True), jnp.sum(total[8:], axis=0, keepdims=True)], axis=0
    )
    part[...] = mine
    zb[slot] = mine
    n_zb = fresh()
    for device in line:
        remote(part, zb.at[slot], device, n_zb)

    for c in go_right + go_left + go_mate + side:
        c.wait_recv()
    hop_mate = [
        remote(conds.at[2, 0], conds.at[2, 1], mate), remote(blocks.at[2, 0], blocks.at[2, 1], mate),
        remote(conds.at[4, 0], conds.at[4, 1], mate), remote(blocks.at[4, 0], blocks.at[4, 1], mate),
    ]
    loads[4].wait()
    loads[5].wait()

    lane32 = lax.broadcasted_iota(jnp.int32, (32, LAT), 1)
    low32, high32 = lane32 == 0, lane32 == LAT - 1
    is_low = ((1 - h).astype(F32), h.astype(F32))
    is_high = (h.astype(F32), (1 - h).astype(F32))

    def north(d, c):
        return conds[d + 3, c, 0] * jnp.where(s + d == 0, 0.0, 1.0)

    def south(d, c):
        return conds[d + 3, c, 1] * jnp.where(s + d == ring - 1, 0.0, 1.0)

    def widen(source, target, level):
        there = lambda d, c: abs(d) <= level - c
        for c in (0, 1):
            for d in range(c - level - 1, level + 2 - c):
                for i in range(0, LAT, 32):
                    rows = pl.ds(i, 32)
                    terms = []
                    if there(d + 1, c):
                        terms.append(source(d + 1, c)[rows] * north(d + 1, c))
                    if there(d - 1, c):
                        terms.append(source(d - 1, c)[rows] * south(d - 1, c))
                    w, e = None, None
                    if there(d, c):
                        me = source(d, c)[rows]
                        w, e = me * conds[d + 3, c, 2], me * conds[d + 3, c, 3]
                    if there(d, 1 - c):
                        ot = source(d, 1 - c)[rows]
                        zero = jnp.zeros_like(ot)
                        w = jnp.where(low32, ot * (conds[d + 3, 1 - c, 2] * is_low[c]), zero if w is None else w)
                        e = jnp.where(high32, ot * (conds[d + 3, 1 - c, 3] * is_high[c]), zero if e is None else e)
                    elif w is not None:
                        w, e = jnp.where(low32, 0.0, w), jnp.where(high32, 0.0, e)
                    if w is not None:
                        terms += [pltpu.roll(w, LAT - 1, 1), pltpu.roll(e, 1, 1)]
                    k_hi, k_lo = split2(sum(terms[1:], terms[0]))
                    kk[rows, :] = jnp.concatenate([k_hi, k_hi, k_lo], axis=1)
                b_hi, b_lo = split2(blocks[d + 3, c])
                q = jnp.dot(kk[...], jnp.concatenate([b_hi, b_lo, b_hi], axis=0), preferred_element_type=F32)
                if target is not None:
                    target[d + 3, c] = q
                if there(d, c):
                    green[d + 3, c] += q
                else:
                    green[d + 3, c] = q

    green[3, 0] = blocks[3, 0]
    widen(lambda d, c: blocks.at[d + 3, c], qb, 0)
    for c in hop_right + hop_left:
        c.wait_recv()
    end_right = [remote(blocks.at[1, 0], blocks.at[0, 0], right)]
    end_left = [remote(blocks.at[5, 0], blocks.at[6, 0], left)]
    end_mate = [remote(blocks.at[1, 0], blocks.at[1, 1], mate), remote(blocks.at[5, 0], blocks.at[5, 1], mate)]
    row128 = lax.broadcasted_iota(jnp.int32, (LAT, LAT), 0)
    lane128 = lax.broadcasted_iota(jnp.int32, (LAT, LAT), 1)
    pick = jnp.where(lane128 == row128 + (z - REACH), 1.0, 0.0).astype(BF16)
    landed(zb.at[pl.ds(0, 15)], n_zb)
    columns = jnp.concatenate([zb[2 * k] + zb[2 * k + 1] for k in range(NZ)], axis=0)
    p_hi, p_lo = split2(columns)
    seven = nt(pick, p_hi) + nt(pick, p_lo)
    seven = jnp.concatenate([seven, jnp.zeros((LAT, LAT - 16), F32)], axis=1)
    a1s[...] = pltpu.roll(seven, (xy % 8) * 16, 1).reshape(NXY, 8, LAT)
    n_a1 = fresh()
    for to, device in plane:
        remote(a1s.at[to], a1.at[xy], device, n_a1)
    a1[xy] = a1s[xy]


    for c in hop_mate:
        c.wait_recv()
    widen(lambda d, c: qb.at[d + 3, c], qa, 1)
    radial_pass(xr, acc)
    for c in copies:
        c.wait_recv()
    lon_pass(xt, acct)

    def section_one(l, carry):
        for v in range(8):
            yr[v, l + 2] = xr[v, l + 2] - (0.5 * TIME_STEP) * (acc[v, l] + acct[v, :, l, :])
        return carry

    lax.fori_loop(0, R, section_one, 0)
    for v in range(8):
        turn(yt, yr, v)
        e = yr[v, 2 + 15 * h]
        yr[v, edge] = e
        yr[v, edge + 1] = e
    again = [
        remote(yr.at[:, pl.ds(2 + low, 2)], yr.at[:, pl.ds(edge, 2)], mate),
        remote(yt.at[:, pl.ds(8, 2)], yt.at[:, pl.ds(0, 2)], right),
        remote(yt.at[:, pl.ds(2, 2)], yt.at[:, pl.ds(10, 2)], left),
    ]
    for c in end_right + end_left + end_mate:
        c.wait_recv()
    widen(lambda d, c: qa.at[d + 3, c], None, 2)

    landed(a1.at[pl.ds(0, 15)], n_a1)
    out = jnp.zeros((LAT, LAT), F32)
    for c in (0, 1):
        first_source = 8 * h if c == 0 else 8 * (1 - h)
        rows = a1[first_source]
        for k in range(1, 8):
            rows = rows + a1[first_source + k]
        for d in range(c - REACH, REACH + 1 - c):
            out = out + green[d + 3, c] * jnp.broadcast_to(rows[d + 3 : d + 4], (LAT, LAT))
    o_hi, o_lo = split2(out)
    all_ones = jnp.ones((16, LAT), BF16)
    potential = (nt(all_ones, o_hi) + nt(all_ones, o_lo))[:1]
    out_pot[...] = potential
    prow[...] = potential
    zp[slot] = potential
    n_zp = fresh()
    for device in line:
        remote(prow, zp.at[slot], device, n_zp)

    lat_pass(yr, 2, acc)

    m = lax.broadcasted_iota(jnp.int32, (2 * NXY, 2 * LAT), 0)
    n = lax.broadcasted_iota(jnp.int32, (2 * NXY, 2 * LAT), 1)
    pick2 = jnp.where(
        n == 2 * (jnp.right_shift(m, 1) * NZ + z) + jnp.bitwise_and(m, 1), 1.0, 0.0
    ).astype(BF16)
    landed(zp.at[pl.ds(0, 15)], n_zp)
    lines = jnp.concatenate(
        [jnp.concatenate([zp[2 * k], zp[2 * k + 1]], axis=1) for k in range(NZ)], axis=0
    )
    l_hi, l_lo = split2(lines)
    picked = nt(pick2, l_hi) + nt(pick2, l_lo)
    picked = jnp.concatenate([picked, jnp.zeros((2 * NXY, LAT - NZ), F32)], axis=1)
    picked = pltpu.roll(picked, xy * NZ, 1)
    for k in range(NXY):
        a2s[k] = picked[2 * k : 2 * k + 2]
    n_a2 = fresh()
    for to, device in plane:
        remote(a2s.at[to], a2.at[xy], device, n_a2)
    a2[xy] = a2s[xy]

    for c in again:
        c.wait_recv()
    radial_pass(yr, acc)
    lon_pass(yt, acct)

    def last_step(l, carry):
        for v in range(8):
            out_state[v, l] = 0.5 * (
                xr[v, l + 2] + yr[v, l + 2] - (0.5 * TIME_STEP) * (acc[v, l] + acct[v, :, l, :])
            )
        return carry

    lax.fori_loop(0, R, last_step, 0)

    landed(a2.at[pl.ds(0, 15)], n_a2)
    table = a2[0]
    for k in range(1, NXY):
        table = table + a2[k]
    out_table[...] = table

    for c in (
        near + copies + side + again + go_right + go_left + go_mate + hop_right + hop_left + hop_mate
        + end_right + end_left + end_mate
    ):
        c.wait_send()
    sent(zb.at[pl.ds(0, 15)], n_zb)
    sent(a1.at[pl.ds(0, 15)], n_a1)
    sent(zp.at[pl.ds(0, 15)], n_zp)
    sent(a2.at[pl.ds(0, 15)], n_a2)
    assert count[0] <= N_SEMS, count[0]


def finish(state, pot, table, foot, out_state, out_pot, out_foot, buf, sem):
    copies = [
        pltpu.make_async_copy(state, out_state, sem.at[0]),
        pltpu.make_async_copy(pot, out_pot, sem.at[1]),
    ]
    for c in copies:
        c.start()
    tab0 = jnp.broadcast_to(table[0:1, :], (LON, LAT))
    tab1 = jnp.broadcast_to(table[1:2, :], (LON, LAT))
    for l in range(R):
        node = foot[l]
        row = jnp.right_shift(node, 8)
        buf[l] = jnp.where(
            jnp.bitwise_and(node, 1) == 0,
            jnp.take_along_axis(tab0, row, axis=1, mode="promise_in_bounds"),
            jnp.take_along_axis(tab1, row, axis=1, mode="promise_in_bounds"),
        )
    copies.append(pltpu.make_async_copy(buf, out_foot, sem.at[2]))
    copies[2].start()
    for c in copies:
        c.wait()


N_SEMS = 52


def body(state, footpoints, conductance, inverse_blocks):
    vmem = pl.BlockSpec(memory_space=pltpu.VMEM)
    hbm = pl.BlockSpec(memory_space=pltpu.HBM)
    whole = (
        jax.ShapeDtypeStruct((8, R, LON, LAT), F32),
        jax.ShapeDtypeStruct((1, LAT), F32),
    )
    cells, potential, table = pl.pallas_call(
        kernel,
        out_shape=whole + (jax.ShapeDtypeStruct((2, LAT), F32),),
        in_specs=[hbm] * 4,
        out_specs=(vmem, vmem, vmem),
        scratch_shapes=[
            pltpu.VMEM((R, LON, LAT), jnp.int32),
            pltpu.VMEM((8, R + 4, LON, LAT), F32),
            pltpu.VMEM((8, LON + 4, R, LAT), F32),
            pltpu.VMEM((8, R + 4, LON, LAT), F32),
            pltpu.VMEM((8, LON + 4, R, LAT), F32),
            pltpu.VMEM((8, R, LON, LAT), F32),
            pltpu.VMEM((8, LON, R, LAT), F32),
            pltpu.VMEM((2, LON, R, LAT), F32),
            pltpu.VMEM((2, 2, R, LAT), F32),
            pltpu.VMEM((2, LAT), F32),
            pltpu.VMEM((16, 2, LAT), F32),
            pltpu.VMEM((NXY, 8, LAT), F32),
            pltpu.VMEM((NXY, 8, LAT), F32),
            pltpu.VMEM((1, LAT), F32),
            pltpu.VMEM((16, 1, LAT), F32),
            pltpu.VMEM((NXY, 2, LAT), F32),
            pltpu.VMEM((NXY, 2, LAT), F32),
            pltpu.VMEM((7, 2, LAT, LAT), F32),
            pltpu.VMEM((7, 2, 4, 1, LAT), F32),
            pltpu.VMEM((7, 2, LAT, LAT), F32),
            pltpu.VMEM((7, 2, LAT, LAT), F32),
            pltpu.VMEM((7, 2, LAT, LAT), F32),
            pltpu.VMEM((LAT, 3 * LAT), BF16),
            pltpu.SemaphoreType.DMA((N_SEMS,)),
            pltpu.SemaphoreType.DMA((N_SEMS,)),
            pltpu.SemaphoreType.DMA((6,)),
        ],
        compiler_params=pltpu.CompilerParams(
            collective_id=0, has_side_effects=True, vmem_limit_bytes=40 << 20
        ),
    )(*(pltpu.with_memory_space_constraint(a, pltpu.HBM) for a in (state, footpoints, conductance, inverse_blocks)))
    return pl.pallas_call(
        finish,
        out_shape=whole + (jax.ShapeDtypeStruct((R, LON, LAT), F32),),
        in_specs=[vmem] * 4,
        out_specs=(hbm, hbm, hbm),
        scratch_shapes=[pltpu.VMEM((R, LON, LAT), F32), pltpu.SemaphoreType.DMA((3,))],
        compiler_params=pltpu.CompilerParams(vmem_limit_bytes=8 << 20),
    )(cells, potential, table, footpoints)


def solution(mesh):
    return jax.shard_map(
        body,
        mesh=mesh,
        in_specs=(
            P(None, "radial", "shell", None),
            P("radial", "shell", None),
            P(None, "shell", "radial"),
            P("shell", "radial", None, None),
        ),
        out_specs=(
            P(None, "radial", "shell", None),
            P("shell", "radial"),
            P("radial", "shell", None),
        ),
        check_vma=False,
    )
```
